32 devices in a mesh: row: 8 (over y, x, core), col: 4 (over z).
Axes of the slice: x: 2, y: 2, z: 4, core: 2. Of those that a mesh axis runs over, the one named last changes fastest.
Arguments:
- alpha_prev: float32 [48, 4096], P(None, 'row'), may hold values from 0.1 to 10
- tokens: int32 [48], replicated, may hold values from 0 to 16639
- src_emb: bfloat16 [4096, 256], P('row'), may hold values from -10 to 10
- dst_emb: bfloat16 [256, 4096], P(None, ('row', 'col')), may hold values from -7 to 7
- emission: bfloat16 [16640, 4096], P(None, ('row', 'col')), may hold values from 0.02 to 8, as said below
Outputs:
- next_alpha: float32 [48, 4096], P(None, 'row')
- log_total: float32 [48], replicated
The draws below stay inside these ranges and needn't reach their ends.
Inputs may be any that keep to these rules, and one draw needn't show every extreme that they name: `emission`: every weight is positive.
All inputs are finite; a program needn't handle non-finite values.
Results may differ from the reference program's by a relative error of at most 0.0014.
Values may be sent and summed in bfloat16 or wider, within the bound.
No kernel may reach another device: no remote copies, remote signals or barrier semaphores. Data moves between devices by JAX's collectives and lax.ppermute only.
A program may use at most 128 MiB of HBM per device.

```python
import math
import jax
import jax.numpy as jnp
import numpy as np
from jax import lax

E = 256
GROUP = 128
V = 16640
B = 48
S = 4096


def embed_pair(key):
    base = jax.random.fold_in(key, 17)
    key_dst, key_col, key_row, key_src = jax.random.split(base, 4)
    dst_table = jnp.clip(jax.random.normal(key_dst, (E, S), jnp.float32), -5.0, 5.0)
    col_scale = jnp.exp(jax.random.uniform(key_col, (S,), jnp.float32, -0.2, 0.2))
    dst_table = dst_table * col_scale[None, :]
    row_scale = jnp.exp(jax.random.uniform(key_row, (S,), jnp.float32, 0.0, 0.7))
    src_table = jnp.clip(jax.random.normal(key_src, (S, E), jnp.float32), -5.0, 5.0) * (3.0 / math.sqrt(E)) * row_scale[:, None]
    return (src_table, dst_table)


def draw_src_emb(key, part):
    return embed_pair(key)[0].astype(jnp.bfloat16)


def draw_dst_emb(key, part):
    return embed_pair(key)[1].astype(jnp.bfloat16)


def draw_emission(key, part):
    base = jax.random.fold_in(key, 29)
    ramp = 1.0 + 3.0 * jnp.arange(S, dtype=jnp.float32) / S
    value = jnp.exp(jax.random.uniform(base, (V, S), jnp.float32, math.log(0.02), 0.0)) * ramp[None, :]
    return value.astype(jnp.bfloat16)


def set_ends(result, key, least, largest):
    longest = result.shape.index(max(result.shape))
    spots = []
    for shift in (0, 1):
        where = [jax.random.randint(jax.random.fold_in(key, axis), (), 0, length) for axis, length in enumerate(result.shape)]
        where[longest] = (where[longest] + shift) % result.shape[longest]
        spots.append(tuple(where))
    return result.at[spots[0]].set(least).at[spots[1]].set(largest)


def block_scale(own_key, dims, cuts, smallest, top_value):
    factor_of = 1.0
    for dim, shards_of in cuts:
        heights = jax.random.uniform(jax.random.fold_in(jax.random.fold_in(own_key, 6), dim), (shards_of,), jnp.float32, smallest / len(cuts), top_value / len(cuts))
        factor_of = factor_of * jnp.repeat(jnp.exp(heights), dims[dim] // shards_of).reshape((-1,) + (1,) * (len(dims) - 1 - dim))
    return factor_of


def rank_bounds(number_of, skew):
    portions = [(1 << 20) // math.isqrt(rank ** skew) + 1 for rank in range(1, number_of + 1)]
    deviation = 1 + sum(portions) // (1 << 30)
    return np.cumsum(np.array([max(1, weight // deviation) for weight in portions]))


def ranked_ids(key, dims, number_of, skew):
    table = rank_bounds(number_of, skew)
    ticket = jax.random.randint(jax.random.fold_in(key, 1), dims, 0, int(table[number_of - 1]))
    grade = jnp.searchsorted(jnp.asarray(table, jnp.int32), ticket, side="right")
    return jax.random.permutation(jax.random.fold_in(key, 2), number_of)[grade].astype(jnp.int32)


def setup_inputs(seed: int = 0) -> dict:
    key_of = jax.random.split(jax.random.key(seed), 6)
    return {
        "alpha_prev": jnp.clip(jnp.exp(math.log(10.0) - 4.6051702 * jax.random.uniform(key_of[0], (B, S), jnp.float32) ** block_scale(key_of[0], (B, S), ((1, 8),), -0.2, 0.2)), 0.1, 10.0),
        "tokens": set_ends(ranked_ids(key_of[1], (B,), V, 2), jax.random.fold_in(key_of[1], 3), 0, V - 1).astype(jnp.int32),
        "src_emb": draw_src_emb(jax.random.fold_in(key_of[5], 71), 0),
        "dst_emb": draw_dst_emb(jax.random.fold_in(key_of[5], 71), 0),
        "emission": draw_emission(jax.random.fold_in(key_of[5], 71), 0),
    }


def reference(alpha_prev, tokens, src_emb, dst_emb, emission):
    states = S
    group_count = states // GROUP
    block_rows = math.gcd(states, 512)

    def absorb(carried, block_index):
        first_row = (block_index * block_rows).astype(jnp.int32)
        src_block = lax.dynamic_slice_in_dim(src_emb, first_row, block_rows, 0)
        alpha_block = lax.dynamic_slice_in_dim(alpha_prev, first_row, block_rows, 1)
        logits = jnp.dot(src_block, dst_emb, preferred_element_type=jnp.float32).reshape(block_rows, group_count, GROUP)
        group_peak = jnp.max(logits, axis=2)
        shifted = jnp.exp(logits - group_peak[:, :, None])
        group_total = jnp.sum(shifted, axis=2)
        expo = shifted.astype(jnp.bfloat16)
        row_peak = jnp.max(group_peak, axis=1)
        row_total = jnp.sum(group_total * jnp.exp(group_peak - row_peak[:, None]), axis=1)
        row_scale = jnp.exp(group_peak - row_peak[:, None]) / row_total[:, None]
        weights = (row_scale.T[:, None, :] * alpha_block[None, :, :]).astype(jnp.bfloat16)
        product = jnp.einsum("gbi,igk->bgk", weights.astype(jnp.float32), expo.astype(jnp.float32))
        return carried + product.reshape(B, states), None

    initial = jnp.zeros((B, states), jnp.float32)
    carried, _ = lax.scan(absorb, initial, jnp.arange(states // block_rows, dtype=jnp.int32))
    emit_rows = jnp.take(emission, tokens, axis=0).astype(jnp.float32)
    emitted = carried * emit_rows
    total = jnp.sum(emitted, axis=1)
    next_alpha = emitted * (states / total)[:, None]
    log_total = jnp.log(total)
    return next_alpha, log_total
```

```python
import functools
import math

import jax
import jax.numpy as jnp
from jax import lax
from jax.experimental import pallas as pl
from jax.experimental.pallas import tpu as pltpu
from jax.sharding import PartitionSpec as P

VMEM = pltpu.MemorySpace.VMEM
SMEM = pltpu.MemorySpace.SMEM
TAIL = 8
CHUNK = 8


def whole(shape):
    return pl.BlockSpec(shape, lambda *_: (0,) * len(shape))


def pick_rows(tokens_ref, table_ref, dst_ref, out_ref, chunks, picked, sem):
    seqs = picked.shape[0]
    depth = dst_ref.shape[0]
    for b in range(seqs):
        first = pl.multiple_of((tokens_ref[b] // CHUNK) * CHUNK, CHUNK)
        pltpu.make_async_copy(
            table_ref.at[pl.ds(first, CHUNK)], chunks.at[pl.ds(b * CHUNK, CHUNK)], sem
        ).start()
    out_ref[:depth] = dst_ref[...]
    pltpu.make_async_copy(table_ref.at[pl.ds(0, seqs * CHUNK)], chunks, sem).wait()
    rows = lax.broadcasted_iota(jnp.int32, (CHUNK, chunks.shape[1]), 0)
    for b in range(seqs):
        chunk = chunks[b * CHUNK : (b + 1) * CHUNK].astype(jnp.float32)
        kept = jnp.where(rows == tokens_ref[b] % CHUNK, chunk, 0.0)
        picked[b : b + 1] = jnp.sum(kept, axis=0, keepdims=True)
    out_ref[depth:] = picked[...].astype(out_ref.dtype)


def softmax_tile(per_step, src_ref, dst_ref, expo_ref, peak_ref, stat_ref, total_ref):
    step = pl.program_id(0)
    depth = src_ref.shape[1]
    for q in range(per_step):
        logits = lax.dot_general(
            dst_ref[q, :depth], src_ref[...], (((0,), (1,)), ((), ())), preferred_element_type=jnp.float32
        )
        peak = jnp.max(logits, axis=0, keepdims=True)
        shifted = jnp.exp(logits - peak)
        slot = pl.ds(step * per_step + q, 1)
        peak_ref[slot] = peak
        total_ref[slot] = jnp.sum(shifted, axis=0, keepdims=True)
        expo_ref[q] = shifted.astype(expo_ref.dtype)

    @pl.when(step == pl.num_programs(0) - 1)
    def _():
        local_peak = jnp.max(peak_ref[...], axis=0, keepdims=True)
        stat_ref[0:1] = local_peak
        stat_ref[1:2] = jnp.sum(total_ref[...] * jnp.exp(peak_ref[...] - local_peak), axis=0, keepdims=True)


def carry_tile(per_step, n_stats, *refs):
    stat_refs = refs[:n_stats]
    alpha_ref, expo_ref, peak_ref, emit_ref, out_ref, spread = refs[n_stats:]
    step = pl.program_id(0)
    seqs = alpha_ref.shape[0]
    depth = emit_ref.shape[1] - seqs

    @pl.when(step == 0)
    def _():
        spread[...] = jnp.zeros_like(spread)

    row_peak = functools.reduce(jnp.maximum, [s[0:1] for s in stat_refs])
    row_total = tree_sum([s[1:2] * jnp.exp(s[0:1] - row_peak) for s in stat_refs])
    for q in range(per_step):
        group = step * per_step + q
        row_scale = jnp.exp(peak_ref[pl.ds(group, 1)] - row_peak) / row_total
        weights = (alpha_ref[...] * row_scale).astype(jnp.bfloat16)
        product = lax.dot_general(
            weights, expo_ref[q], (((1,), (1,)), ((), ())), preferred_element_type=jnp.float32
        )
        out_ref[group, :seqs] = product
        spread[:seqs] += product * emit_ref[q, depth:].astype(jnp.float32)

    @pl.when(step == pl.num_programs(0) - 1)
    def _():
        share = jnp.sum(spread[...].T, axis=0, keepdims=True)
        tail = jnp.broadcast_to(share, (TAIL, share.shape[1]))
        for group in range(out_ref.shape[0]):
            out_ref[group, seqs:] = tail


def tree_sum(terms):
    while len(terms) > 1:
        terms = [a + b for a, b in zip(terms[::2], terms[1::2], strict=True)]
    return terms[0]


def emit_block(parts_ref, own_ref, out_ref):
    seqs = out_ref.shape[0] - TAIL
    sums = jnp.sum(parts_ref[...], axis=0)
    out_ref[:seqs] = sums[:seqs] * own_ref[own_ref.shape[0] - seqs :].astype(jnp.float32)
    out_ref[seqs:] = sums[seqs:]


def finish(states, n_blocks, *refs):
    place_ref = refs[0]
    block_refs = refs[1 : 1 + n_blocks]
    alpha_ref, log_ref = refs[1 + n_blocks :]
    seqs, cols = alpha_ref.shape[0], block_refs[0].shape[1]
    total = tree_sum([b[seqs:] for b in block_refs])
    log_ref[...] = jnp.log(total[0, :seqs])
    scale = (states / jnp.broadcast_to(total[0:1], (cols, cols)).T)[:seqs]
    for k in range(n_blocks):
        start = pl.multiple_of((place_ref[0] ^ k) * cols, cols)
        alpha_ref[:, pl.ds(start, cols)] = block_refs[k][:seqs] * scale


def swap(x, axis, count):
    return [x] + [lax.ppermute(x, axis, [(i, i ^ k) for i in range(count)]) for k in range(1, count)]


def on_device(alpha_prev, tokens, src_emb, dst_emb, emission):
    rows = lax.axis_size("row")
    cols = lax.axis_size("col")
    seqs, sources = alpha_prev.shape
    depth, group = dst_emb.shape
    f32 = jnp.float32

    packed = pl.pallas_call(
        pick_rows,
        out_shape=jax.ShapeDtypeStruct((depth + seqs, group), jnp.bfloat16),
        in_specs=[
            pl.BlockSpec(memory_space=SMEM),
            pl.BlockSpec(memory_space=pl.ANY),
            pl.BlockSpec(memory_space=VMEM),
        ],
        out_specs=pl.BlockSpec(memory_space=VMEM),
        scratch_shapes=[
            pltpu.VMEM((seqs * CHUNK, group), jnp.bfloat16),
            pltpu.VMEM((seqs, group), f32),
            pltpu.SemaphoreType.DMA,
        ],
        name="pick_rows",
    )(tokens, emission, dst_emb)

    gathered = lax.all_gather(packed, "row", axis=0)

    per_step = math.gcd(rows, 8)
    steps = rows // per_step
    expo, peak, stat = pl.pallas_call(
        functools.partial(softmax_tile, per_step),
        out_shape=(
            jax.ShapeDtypeStruct((rows, group, sources), jnp.bfloat16),
            jax.ShapeDtypeStruct((rows, sources), f32),
            jax.ShapeDtypeStruct((2, sources), f32),
        ),
        grid=(steps,),
        in_specs=[
            whole((sources, depth)),
            pl.BlockSpec((per_step, depth + seqs, group), lambda s: (s, 0, 0)),
        ],
        out_specs=(
            pl.BlockSpec((per_step, group, sources), lambda s: (s, 0, 0)),
            whole((rows, sources)),
            whole((2, sources)),
        ),
        scratch_shapes=[pltpu.VMEM((rows, sources), f32)],
        name="softmax_tile",
    )(src_emb, gathered)

    stats = swap(stat, "col", cols)
    partial = pl.pallas_call(
        functools.partial(carry_tile, per_step, cols),
        out_shape=jax.ShapeDtypeStruct((rows, seqs + TAIL, group), f32),
        grid=(steps,),
        in_specs=[whole((2, sources))] * cols
        + [
            whole((seqs, sources)),
            pl.BlockSpec((per_step, group, sources), lambda s: (s, 0, 0)),
            whole((rows, sources)),
            pl.BlockSpec((per_step, depth + seqs, group), lambda s: (s, 0, 0)),
        ],
        out_specs=whole((rows, seqs + TAIL, group)),
        scratch_shapes=[pltpu.VMEM((group, group), f32)],
        name="carry_tile",
    )(*stats, alpha_prev, expo, peak, gathered)

    parts = lax.all_to_all(partial, "row", 0, 0)
    block = pl.pallas_call(
        emit_block,
        out_shape=jax.ShapeDtypeStruct((seqs + TAIL, group), f32),
        in_specs=[pl.BlockSpec(memory_space=VMEM)] * 2,
        out_specs=pl.BlockSpec(memory_space=VMEM),
        name="emit_block",
    )(parts, packed)

    blocks = swap(block, "col", cols)
    place = lax.axis_index("col").astype(jnp.int32).reshape(1)
    return pl.pallas_call(
        functools.partial(finish, float(group * rows * cols), cols),
        out_shape=(jax.ShapeDtypeStruct((seqs, group * cols), f32), jax.ShapeDtypeStruct((seqs,), f32)),
        in_specs=[pl.BlockSpec(memory_space=SMEM)] + [pl.BlockSpec(memory_space=VMEM)] * cols,
        out_specs=(pl.BlockSpec(memory_space=VMEM), pl.BlockSpec(memory_space=VMEM)),
        name="finish",
    )(place, *blocks)


def solution(mesh):
    placed = (P(None, "row"), P(), P("row", None), P(None, ("row", "col")), P(None, ("row", "col")))
    return jax.shard_map(
        on_device, mesh=mesh, in_specs=placed, out_specs=(P(None, "row"), P()), check_vma=False
    )
```

```python
import functools
import math

import jax
import jax.numpy as jnp
from jax import lax
from jax.experimental import pallas as pl
from jax.experimental.pallas import tpu as pltpu
from jax.sharding import PartitionSpec as P

VMEM = pltpu.MemorySpace.VMEM
SMEM = pltpu.MemorySpace.SMEM
HBM = pltpu.MemorySpace.HBM
TAIL = 8
CHUNK = 8


def room(mebibytes):
    return pltpu.CompilerParams(vmem_limit_bytes=mebibytes << 20)


def block_specs(steps, shapes):
    if steps == 1:
        return [pl.BlockSpec(memory_space=VMEM) for _ in shapes]
    return [
        pl.BlockSpec(shape, lambda s, n=len(shape), moves=moves: (s if moves else 0,) + (0,) * (n - 1))
        for shape, moves in shapes
    ]


def pick_rows(tokens_ref, table_ref, dst_ref, out_ref, chunks, picked, sem):
    seqs = picked.shape[0]
    depth = dst_ref.shape[0]
    for b in range(seqs):
        first = pl.multiple_of((tokens_ref[b] // CHUNK) * CHUNK, CHUNK)
        pltpu.make_async_copy(
            table_ref.at[pl.ds(first, CHUNK)], chunks.at[pl.ds(b * CHUNK, CHUNK)], sem
        ).start()
    out_ref[:depth] = dst_ref[...]
    pltpu.make_async_copy(table_ref.at[pl.ds(0, seqs * CHUNK)], chunks, sem).wait()
    rows = lax.broadcasted_iota(jnp.int32, (CHUNK, chunks.shape[1]), 0)
    for b in range(seqs):
        chunk = chunks[b * CHUNK : (b + 1) * CHUNK].astype(jnp.float32)
        kept = jnp.where(rows == tokens_ref[b] % CHUNK, chunk, 0.0)
        picked[b : b + 1] = jnp.sum(kept, axis=0, keepdims=True)
    out_ref[depth:] = picked[...].astype(out_ref.dtype)


def softmax_tile(steps, per_step, src_ref, dst_ref, expo_ref, peak_ref, stat_ref, total_ref):
    step = pl.program_id(0) if steps > 1 else 0
    depth = src_ref.shape[1]
    for q in range(per_step):
        logits = lax.dot_general(
            dst_ref[q, :depth], src_ref[...], (((0,), (1,)), ((), ())), preferred_element_type=jnp.float32
        )
        peak = jnp.max(logits, axis=0, keepdims=True)
        shifted = jnp.exp(logits - peak)
        slot = pl.ds(step * per_step + q, 1)
        peak_ref[slot] = peak
        total_ref[slot] = jnp.sum(shifted, axis=0, keepdims=True)
        expo_ref[q] = shifted.astype(expo_ref.dtype)

    @pl.when(step == steps - 1)
    def _():
        local_peak = jnp.max(peak_ref[...], axis=0, keepdims=True)
        stat_ref[0:1] = local_peak
        stat_ref[1:2] = jnp.sum(total_ref[...] * jnp.exp(peak_ref[...] - local_peak), axis=0, keepdims=True)


def carry_tile(steps, per_step, n_stats, *refs):
    stat_refs = refs[:n_stats]
    alpha_ref, expo_ref, peak_ref, emit_ref, out_ref, spread = refs[n_stats:]
    step = pl.program_id(0) if steps > 1 else 0
    seqs = alpha_ref.shape[0]
    depth = emit_ref.shape[1] - seqs

    @pl.when(step == 0)
    def _():
        spread[...] = jnp.zeros_like(spread)

    row_peak = functools.reduce(jnp.maximum, [s[0:1] for s in stat_refs])
    row_total = tree_sum([s[1:2] * jnp.exp(s[0:1] - row_peak) for s in stat_refs])
    for q in range(per_step):
        group = step * per_step + q
        row_scale = jnp.exp(peak_ref[pl.ds(group, 1)] - row_peak) / row_total
        weights = (alpha_ref[...] * row_scale).astype(jnp.bfloat16)
        product = lax.dot_general(
            weights, expo_ref[q], (((1,), (1,)), ((), ())), preferred_element_type=jnp.float32
        )
        out_ref[group, :seqs] = product
        spread[:seqs] += product * emit_ref[q, depth:].astype(jnp.float32)

    @pl.when(step == steps - 1)
    def _():
        share = jnp.sum(spread[...].T, axis=0, keepdims=True)
        tail = jnp.broadcast_to(share, (TAIL, share.shape[1]))
        for group in range(out_ref.shape[0]):
            out_ref[group, seqs:] = tail


def tree_sum(terms):
    while len(terms) > 1:
        terms = [a + b for a, b in zip(terms[::2], terms[1::2], strict=True)]
    return terms[0]


def emit_block(parts_ref, own_ref, out_ref):
    seqs = out_ref.shape[0] - TAIL
    sums = jnp.sum(parts_ref[...], axis=0)
    out_ref[:seqs] = sums[:seqs] * own_ref[own_ref.shape[0] - seqs :].astype(jnp.float32)
    out_ref[seqs:] = sums[seqs:]


def finish(states, n_blocks, *refs):
    place_ref = refs[0]
    block_refs = refs[1 : 1 + n_blocks]
    alpha_ref, log_ref = refs[1 + n_blocks :]
    seqs, cols = alpha_ref.shape[0], block_refs[0].shape[1]
    total = tree_sum([b[seqs:] for b in block_refs])
    log_ref[...] = jnp.log(total[0, :seqs])
    scale = (states / jnp.broadcast_to(total[0:1], (cols, cols)).T)[:seqs]
    for k in range(n_blocks):
        start = pl.multiple_of((place_ref[0] ^ k) * cols, cols)
        alpha_ref[:, pl.ds(start, cols)] = block_refs[k][:seqs] * scale


def swap(x, axis, count):
    return [x] + [lax.ppermute(x, axis, [(i, i ^ k) for i in range(count)]) for k in range(1, count)]


def on_device(alpha_prev, tokens, src_emb, dst_emb, emission):
    rows = lax.axis_size("row")
    cols = lax.axis_size("col")
    seqs, sources = alpha_prev.shape
    depth, group = dst_emb.shape
    f32 = jnp.float32

    packed = pl.pallas_call(
        pick_rows,
        out_shape=jax.ShapeDtypeStruct((depth + seqs, group), jnp.bfloat16),
        in_specs=[
            pl.BlockSpec(memory_space=SMEM),
            pl.BlockSpec(memory_space=HBM),
            pl.BlockSpec(memory_space=VMEM),
        ],
        out_specs=pl.BlockSpec(memory_space=VMEM),
        scratch_shapes=[
            pltpu.VMEM((seqs * CHUNK, group), jnp.bfloat16),
            pltpu.VMEM((seqs, group), f32),
            pltpu.SemaphoreType.DMA,
        ],
        name="pick_rows",
        compiler_params=room(8),
    )(tokens, pltpu.with_memory_space_constraint(emission, HBM), dst_emb)

    gathered = lax.all_gather(packed, "row", axis=0)

    per_step = math.gcd(rows, 8)
    steps = rows // per_step
    grid = (steps,) if steps > 1 else ()
    arrived = ((per_step, depth + seqs, group), True)
    tile = ((per_step, group, sources), True)
    expo, peak, stat = pl.pallas_call(
        functools.partial(softmax_tile, steps, per_step),
        out_shape=(
            jax.ShapeDtypeStruct((rows, group, sources), jnp.bfloat16),
            jax.ShapeDtypeStruct((rows, sources), f32),
            jax.ShapeDtypeStruct((2, sources), f32),
        ),
        grid=grid,
        in_specs=block_specs(steps, [((sources, depth), False), arrived]),
        out_specs=block_specs(steps, [tile, ((rows, sources), False), ((2, sources), False)]),
        scratch_shapes=[pltpu.VMEM((rows, sources), f32)],
        name="softmax_tile",
        compiler_params=room(16),
    )(src_emb, gathered)

    stats = swap(stat, "col", cols)
    stat_block = ((2, sources), False)
    (partial,) = pl.pallas_call(
        functools.partial(carry_tile, steps, per_step, cols),
        out_shape=(jax.ShapeDtypeStruct((rows, seqs + TAIL, group), f32),),
        grid=grid,
        in_specs=block_specs(
            steps,
            [stat_block] * cols + [((seqs, sources), False), tile, ((rows, sources), False), arrived],
        ),
        out_specs=block_specs(steps, [((rows, seqs + TAIL, group), False)]),
        scratch_shapes=[pltpu.VMEM((group, group), f32)],
        name="carry_tile",
        compiler_params=room(16),
    )(*stats, alpha_prev, expo, peak, gathered)

    parts = lax.all_to_all(partial, "row", 0, 0)
    block = pl.pallas_call(
        emit_block,
        out_shape=jax.ShapeDtypeStruct((seqs + TAIL, group), f32),
        in_specs=[pl.BlockSpec(memory_space=VMEM)] * 2,
        out_specs=pl.BlockSpec(memory_space=VMEM),
        name="emit_block",
        compiler_params=room(8),
    )(parts, packed)

    blocks = swap(block, "col", cols)
    place = lax.axis_index("col").astype(jnp.int32).reshape(1)
    return pl.pallas_call(
        functools.partial(finish, float(group * rows * cols), cols),
        out_shape=(jax.ShapeDtypeStruct((seqs, group * cols), f32), jax.ShapeDtypeStruct((seqs,), f32)),
        in_specs=[pl.BlockSpec(memory_space=SMEM)] + [pl.BlockSpec(memory_space=VMEM)] * cols,
        out_specs=(pl.BlockSpec(memory_space=VMEM), pl.BlockSpec(memory_space=VMEM)),
        name="finish",
        compiler_params=room(8),
    )(place, *blocks)


def solution(mesh):
    placed = (P(None, "row"), P(), P("row", None), P(None, ("row", "col")), P(None, ("row", "col")))
    return jax.shard_map(
        on_device, mesh=mesh, in_specs=placed, out_specs=(P(None, "row"), P()), check_vma=False
    )
```

```python
import functools
import math

import jax
import jax.numpy as jnp
from jax import lax
from jax.experimental import pallas as pl
from jax.experimental.pallas import tpu as pltpu
from jax.sharding import PartitionSpec as P

VMEM = pltpu.MemorySpace.VMEM
SMEM = pltpu.MemorySpace.SMEM
HBM = pltpu.MemorySpace.HBM
TAIL = 8
CHUNK = 8


def room(mebibytes):
    return pltpu.CompilerParams(vmem_limit_bytes=mebibytes << 20)


def block_specs(steps, shapes):
    if steps == 1:
        return [pl.BlockSpec(memory_space=VMEM) for _ in shapes]
    return [
        pl.BlockSpec(shape, lambda s, n=len(shape), moves=moves: (s if moves else 0,) + (0,) * (n - 1))
        for shape, moves in shapes
    ]


def pick_rows(tokens_ref, table_ref, dst_ref, out_ref, ids, chunks, picked, ids_sem, dst_sem, sem):
    seqs = picked.shape[0]
    depth = dst_ref.shape[0]
    ids_copy = pltpu.make_async_copy(tokens_ref, ids, ids_sem)
    dst_copy = pltpu.make_async_copy(dst_ref, out_ref.at[pl.ds(0, depth)], dst_sem)
    ids_copy.start()
    dst_copy.start()
    ids_copy.wait()
    for b in range(seqs):
        first = pl.multiple_of((ids[b] // CHUNK) * CHUNK, CHUNK)
        pltpu.make_async_copy(
            table_ref.at[pl.ds(first, CHUNK)], chunks.at[pl.ds(b * CHUNK, CHUNK)], sem
        ).start()
    pltpu.make_async_copy(table_ref.at[pl.ds(0, seqs * CHUNK)], chunks, sem).wait()
    rows = lax.broadcasted_iota(jnp.int32, (CHUNK, chunks.shape[1]), 0)
    for b in range(seqs):
        chunk = chunks[b * CHUNK : (b + 1) * CHUNK].astype(jnp.float32)
        kept = jnp.where(rows == ids[b] % CHUNK, chunk, 0.0)
        picked[b : b + 1] = jnp.sum(kept, axis=0, keepdims=True)
    out_ref[depth:] = picked[...].astype(out_ref.dtype)
    dst_copy.wait()


def softmax_tile(steps, per_step, src_ref, *refs):
    dst_refs = refs[:-4]
    expo_ref, peak_ref, stat_ref, total_ref = refs[-4:]
    step = pl.program_id(0) if steps > 1 else 0
    depth = src_ref.shape[1]
    for q in range(per_step):
        logits = lax.dot_general(
            nth(dst_refs, q)[:depth], src_ref[...], (((0,), (1,)), ((), ())), preferred_element_type=jnp.float32
        )
        peak = jnp.max(logits, axis=0, keepdims=True)
        shifted = jnp.exp(logits - peak)
        slot = pl.ds(step * per_step + q, 1)
        peak_ref[slot] = peak
        total_ref[slot] = jnp.sum(shifted, axis=0, keepdims=True)
        expo_ref[q] = shifted.astype(expo_ref.dtype)

    @pl.when(step == steps - 1)
    def _():
        local_peak = jnp.max(peak_ref[...], axis=0, keepdims=True)
        stat_ref[0:1] = local_peak
        stat_ref[1:2] = jnp.sum(total_ref[...] * jnp.exp(peak_ref[...] - local_peak), axis=0, keepdims=True)


def carry_tile(steps, per_step, n_stats, n_out, *refs):
    stat_refs = refs[:n_stats]
    alpha_ref, expo_ref, peak_ref = refs[n_stats : n_stats + 3]
    emit_refs = refs[n_stats + 3 : -1 - n_out]
    out_refs = refs[-1 - n_out : -1]
    spread = refs[-1]
    step = pl.program_id(0) if steps > 1 else 0
    seqs = alpha_ref.shape[0]
    each = out_refs[0].shape[0]

    @pl.when(step == 0)
    def _():
        spread[...] = jnp.zeros_like(spread)

    row_peak = functools.reduce(jnp.maximum, [s[0:1] for s in stat_refs])
    row_total = tree_sum([s[1:2] * jnp.exp(s[0:1] - row_peak) for s in stat_refs])
    for q in range(per_step):
        group = step * per_step + q
        row_scale = jnp.exp(peak_ref[pl.ds(group, 1)] - row_peak) / row_total
        weights = (alpha_ref[...] * row_scale).astype(jnp.bfloat16)
        product = lax.dot_general(
            weights, expo_ref[q], (((1,), (1,)), ((), ())), preferred_element_type=jnp.float32
        )
        if steps > 1:
            out_refs[0][group, :seqs] = product
        else:
            out_refs[q // each][q % each, :seqs] = product
        emit_ref = nth(emit_refs, q)
        spread[:seqs] += product * emit_ref[emit_ref.shape[0] - seqs :].astype(jnp.float32)

    @pl.when(step == steps - 1)
    def _():
        share = jnp.sum(spread[...].T, axis=0, keepdims=True)
        tail = jnp.broadcast_to(share, (TAIL, share.shape[1]))
        for out_ref in out_refs:
            for group in range(each):
                out_ref[group, seqs:] = tail


def nth(refs, q):
    return refs[q] if len(refs) > 1 else refs[0].at[q]


def tree_sum(terms):
    while len(terms) > 1:
        terms = [a + b for a, b in zip(terms[::2], terms[1::2], strict=True)]
    return terms[0]


def add_pair(kept_ref, given_ref, *out_refs):
    for m, out_ref in enumerate(out_refs):
        out_ref[...] = kept_ref[m] + given_ref[m]


def emit_block(own_ref, *refs):
    parts_refs, out_ref = refs[:-1], refs[-1]
    seqs = out_ref.shape[0] - TAIL
    if len(parts_refs) > 1:
        sums = tree_sum([r[...] for r in parts_refs])
    else:
        sums = jnp.sum(parts_refs[0][...], axis=0)
    out_ref[:seqs] = sums[:seqs] * own_ref[own_ref.shape[0] - seqs :].astype(jnp.float32)
    out_ref[seqs:] = sums[seqs:]


def finish(states, n_blocks, *refs):
    place_ref = refs[0]
    block_refs = refs[1 : 1 + n_blocks]
    alpha_ref, log_ref = refs[1 + n_blocks :]
    seqs, cols = alpha_ref.shape[0], block_refs[0].shape[1]
    total = tree_sum([b[seqs:] for b in block_refs])
    log_ref[...] = jnp.log(total[0, :seqs])
    scale = (states / jnp.broadcast_to(total[0:1], (cols, cols)).T)[:seqs]
    for k in range(n_blocks):
        start = pl.multiple_of((place_ref[0] ^ k) * cols, cols)
        alpha_ref[:, pl.ds(start, cols)] = block_refs[k][:seqs] * scale


def hop(x, axis, count, k):
    return lax.ppermute(x, axis, [(i, i ^ k) for i in range(count)])


def swap(x, axis, count):
    return [x] + [hop(x, axis, count, k) for k in range(1, count)]


def on_device(alpha_prev, tokens, src_emb, dst_emb, emission):
    rows = lax.axis_size("row")
    cols = lax.axis_size("col")
    seqs, sources = alpha_prev.shape
    depth, group = dst_emb.shape
    f32 = jnp.float32

    packed = pl.pallas_call(
        pick_rows,
        out_shape=jax.ShapeDtypeStruct((depth + seqs, group), jnp.bfloat16),
        in_specs=[pl.BlockSpec(memory_space=HBM)] * 3,
        out_specs=pl.BlockSpec(memory_space=VMEM),
        scratch_shapes=[
            pltpu.SMEM((seqs,), jnp.int32),
            pltpu.VMEM((seqs * CHUNK, group), jnp.bfloat16),
            pltpu.VMEM((seqs, group), f32),
            pltpu.SemaphoreType.DMA,
            pltpu.SemaphoreType.DMA,
            pltpu.SemaphoreType.DMA,
        ],
        name="pick_rows",
        compiler_params=room(8),
    )(*[pltpu.with_memory_space_constraint(x, HBM) for x in (tokens, emission, dst_emb)])

    paired = rows == 8
    if paired:
        like = [packed] + [hop(packed, "row", rows, k) for k in range(2, rows, 2)]
        arrived = like + [hop(x, "row", rows, 1) for x in like]
    else:
        arrived = [lax.all_gather(packed, "row", axis=0)]

    per_step = math.gcd(rows, 8)
    steps = rows // per_step
    grid = (steps,) if steps > 1 else ()
    arrived_blocks = [((per_step, depth + seqs, group), True)] * len(arrived)
    tile = ((per_step, group, sources), True)
    expo, peak, stat = pl.pallas_call(
        functools.partial(softmax_tile, steps, per_step),
        out_shape=(
            jax.ShapeDtypeStruct((rows, group, sources), jnp.bfloat16),
            jax.ShapeDtypeStruct((rows, sources), f32),
            jax.ShapeDtypeStruct((2, sources), f32),
        ),
        grid=grid,
        in_specs=block_specs(steps, [((sources, depth), False)] + arrived_blocks),
        out_specs=block_specs(steps, [tile, ((rows, sources), False), ((2, sources), False)]),
        scratch_shapes=[pltpu.VMEM((rows, sources), f32)],
        name="softmax_tile",
        compiler_params=room(16),
    )(src_emb, *arrived)

    stats = swap(stat, "col", cols)
    stat_block = ((2, sources), False)
    n_out = 2 if paired else 1
    partial = pl.pallas_call(
        functools.partial(carry_tile, steps, per_step, cols, n_out),
        out_shape=(jax.ShapeDtypeStruct((rows // n_out, seqs + TAIL, group), f32),) * n_out,
        grid=grid,
        in_specs=block_specs(
            steps,
            [stat_block] * cols + [((seqs, sources), False), tile, ((rows, sources), False)] + arrived_blocks,
        ),
        out_specs=block_specs(steps, [((rows // n_out, seqs + TAIL, group), False)] * n_out),
        scratch_shapes=[pltpu.VMEM((group, group), f32)],
        name="carry_tile",
        compiler_params=room(16),
    )(*stats, alpha_prev, expo, peak, *arrived)

    if paired:
        given = hop(partial[1], "row", rows, 1)
        sums = pl.pallas_call(
            add_pair,
            out_shape=(jax.ShapeDtypeStruct((seqs + TAIL, group), f32),) * (rows // 2),
            in_specs=[pl.BlockSpec(memory_space=VMEM)] * 2,
            out_specs=(pl.BlockSpec(memory_space=VMEM),) * (rows // 2),
            name="add_pair",
            compiler_params=room(8),
        )(partial[0], given)
        parts = [sums[0]] + [hop(sums[m], "row", rows, 2 * m) for m in range(1, rows // 2)]
    else:
        parts = [lax.all_to_all(partial[0], "row", 0, 0)]
    block = pl.pallas_call(
        emit_block,
        out_shape=jax.ShapeDtypeStruct((seqs + TAIL, group), f32),
        in_specs=[pl.BlockSpec(memory_space=VMEM)] * (1 + len(parts)),
        out_specs=pl.BlockSpec(memory_space=VMEM),
        name="emit_block",
        compiler_params=room(8),
    )(packed, *parts)

    blocks = swap(block, "col", cols)
    place = lax.axis_index("col").astype(jnp.int32).reshape(1)
    return pl.pallas_call(
        functools.partial(finish, float(group * rows * cols), cols),
        out_shape=(jax.ShapeDtypeStruct((seqs, group * cols), f32), jax.ShapeDtypeStruct((seqs,), f32)),
        in_specs=[pl.BlockSpec(memory_space=SMEM)] + [pl.BlockSpec(memory_space=VMEM)] * cols,
        out_specs=(pl.BlockSpec(memory_space=VMEM), pl.BlockSpec(memory_space=VMEM)),
        name="finish",
        compiler_params=room(8),
    )(place, *blocks)


def solution(mesh):
    placed = (P(None, "row"), P(), P("row", None), P(None, ("row", "col")), P(None, ("row", "col")))
    return jax.shard_map(
        on_device, mesh=mesh, in_specs=placed, out_specs=(P(None, "row"), P()), check_vma=False
    )
```

```python
import functools
import math

import jax
import jax.numpy as jnp
from jax import lax
from jax.experimental import pallas as pl
from jax.experimental.pallas import tpu as pltpu
from jax.sharding import PartitionSpec as P

VMEM = pltpu.MemorySpace.VMEM
SMEM = pltpu.MemorySpace.SMEM
HBM = pltpu.MemorySpace.HBM
TAIL = 8
CHUNK = 8


def room(mebibytes):
    return pltpu.CompilerParams(vmem_limit_bytes=mebibytes << 20)


def block_specs(steps, shapes):
    if steps == 1:
        return [pl.BlockSpec(memory_space=VMEM) for _ in shapes]
    return [
        pl.BlockSpec(shape, lambda s, n=len(shape), moves=moves: (s if moves else 0,) + (0,) * (n - 1))
        for shape, moves in shapes
    ]


def pick_rows(tokens_ref, table_ref, dst_ref, out_ref, ids, chunks, picked, ids_sem, dst_sem, sem):
    seqs = picked.shape[0]
    depth = dst_ref.shape[0]
    ids_copy = pltpu.make_async_copy(tokens_ref, ids, ids_sem)
    dst_copy = pltpu.make_async_copy(dst_ref, out_ref.at[pl.ds(0, depth)], dst_sem)
    ids_copy.start()
    dst_copy.start()
    ids_copy.wait()
    for b in range(seqs):
        first = pl.multiple_of((ids[b] // CHUNK) * CHUNK, CHUNK)
        pltpu.make_async_copy(
            table_ref.at[pl.ds(first, CHUNK)], chunks.at[pl.ds(b * CHUNK, CHUNK)], sem
        ).start()
    pltpu.make_async_copy(table_ref.at[pl.ds(0, seqs * CHUNK)], chunks, sem).wait()
    rows = lax.broadcasted_iota(jnp.int32, (CHUNK, chunks.shape[1]), 0)
    for b in range(seqs):
        chunk = chunks[b * CHUNK : (b + 1) * CHUNK].astype(jnp.float32)
        kept = jnp.where(rows == ids[b] % CHUNK, chunk, 0.0)
        picked[b : b + 1] = jnp.sum(kept, axis=0, keepdims=True)
    out_ref[depth:] = picked[...].astype(out_ref.dtype)
    dst_copy.wait()


def merge(first, second):
    peak = jnp.maximum(first[0], second[0])
    return peak, first[1] * jnp.exp(first[0] - peak) + second[1] * jnp.exp(second[0] - peak)


def softmax_tile(steps, per_step, n_src, n_dst, *refs):
    src_refs, dst_refs = refs[:n_src], pieces(refs[n_src : n_src + n_dst])
    earlier = refs[n_src + n_dst : -3]
    expo_ref, peak_ref, stat_ref = refs[-3:]
    step = pl.program_id(0) if steps > 1 else 0
    depth = src_refs[0].shape[1]
    for h, src_ref in enumerate(src_refs):
        lanes = slice(h * src_ref.shape[0], (h + 1) * src_ref.shape[0])
        stats = []
        for q in range(per_step):
            logits = lax.dot_general(
                dst_refs[q][:depth], src_ref[...], (((0,), (1,)), ((), ())), preferred_element_type=jnp.float32
            )
            peak = jnp.max(logits, axis=0, keepdims=True)
            shifted = jnp.exp(logits - peak)
            peak_ref[pl.ds(step * per_step + q, 1), lanes] = peak
            stats.append((peak, jnp.sum(shifted, axis=0, keepdims=True)))
            expo_ref[q, :, lanes] = shifted.astype(expo_ref.dtype)
        local_peak = functools.reduce(jnp.maximum, [p for p, _ in stats])
        local_total = functools.reduce(jnp.add, [t * jnp.exp(p - local_peak) for p, t in stats])

        def put(pair, lanes=lanes):
            stat_ref[0:1, lanes], stat_ref[1:2, lanes] = pair

        if earlier:
            put(merge((local_peak, local_total), (earlier[0][0:1, lanes], earlier[0][1:2, lanes])))
        elif steps == 1:
            put((local_peak, local_total))
        else:

            @pl.when(step == 0)
            def _(put=put, pair=(local_peak, local_total)):
                put(pair)

            @pl.when(step > 0)
            def _(put=put, pair=(local_peak, local_total), lanes=lanes):
                put(merge((stat_ref[0:1, lanes], stat_ref[1:2, lanes]), pair))


def carry_tile(steps, per_step, n_stats, n_src, n_tiles, n_out, *refs):
    stat_refs, refs = refs[:n_stats], refs[n_stats:]
    alpha_refs, refs = refs[:n_src], refs[n_src:]
    expo_refs, refs = refs[:n_tiles], refs[n_tiles:]
    peak_refs, refs = refs[:n_tiles], refs[n_tiles:]
    emit_refs, out_refs, spread = pieces(refs[: -1 - n_out]), refs[-1 - n_out : -1], refs[-1]
    step = pl.program_id(0) if steps > 1 else 0
    seqs, sources = alpha_refs[0].shape
    each = per_step // n_tiles

    @pl.when(step == 0)
    def _():
        spread[...] = jnp.zeros_like(spread)

    scales = []
    for h in range(n_src):
        lanes = slice(h * sources, (h + 1) * sources)
        row_peak = functools.reduce(jnp.maximum, [s[0:1, lanes] for s in stat_refs])
        scales.append((lanes, row_peak, tree_sum([s[1:2, lanes] * jnp.exp(s[0:1, lanes] - row_peak) for s in stat_refs])))
    shares = []
    for t in range(n_tiles):
        terms = []
        for i in range(each):
            slot = step * each + i
            product = []
            for alpha_ref, (lanes, row_peak, row_total) in zip(alpha_refs, scales, strict=True):
                row_scale = jnp.exp(peak_refs[t][pl.ds(slot, 1), lanes] - row_peak) / row_total
                weights = (alpha_ref[...] * row_scale).astype(jnp.bfloat16)
                product.append(
                    lax.dot_general(
                        weights,
                        expo_refs[t][i, :, lanes],
                        (((1,), (1,)), ((), ())),
                        preferred_element_type=jnp.float32,
                    )
                )
            product = tree_sum(product)
            if len(out_refs[0].shape) == 3:
                out_refs[0][slot, :seqs] = product
            elif t == 0:
                out_refs[i][:seqs] = product
            emit_ref = emit_refs[t * each + i]
            terms.append(product * emit_ref[emit_ref.shape[0] - seqs :].astype(jnp.float32))
        shares.append(functools.reduce(jnp.add, terms))
    spread[:seqs] += tree_sum(shares)

    @pl.when(step == steps - 1)
    def _():
        share = jnp.sum(spread[...].T, axis=0, keepdims=True)
        tail = jnp.broadcast_to(share, (TAIL, share.shape[1]))
        for out_ref in out_refs:
            if len(out_ref.shape) == 3:
                for group in range(out_ref.shape[0]):
                    out_ref[group, seqs:] = tail
            else:
                out_ref[seqs:] = tail


def pieces(refs):
    views = [[r.at[i] for i in range(r.shape[0])] if len(r.shape) == 3 else [r] for r in refs]
    return sum(views, [])


def stack(*refs):
    for i, ref in enumerate(refs[:-1]):
        refs[-1][i] = ref[...]


def tree_sum(terms):
    while len(terms) > 1:
        terms = [a + b for a, b in zip(terms[::2], terms[1::2], strict=True)]
    return terms[0]


def emit_block(own_ref, *refs):
    parts_refs, out_ref = refs[:-1], refs[-1]
    seqs = out_ref.shape[0] - TAIL
    if len(parts_refs) > 1:
        sums = tree_sum([r[...] for r in parts_refs])
    else:
        sums = jnp.sum(parts_refs[0][...], axis=0)
    out_ref[:seqs] = sums[:seqs] * own_ref[own_ref.shape[0] - seqs :].astype(jnp.float32)
    out_ref[seqs:] = sums[seqs:]


def finish(states, n_blocks, *refs):
    place_ref = refs[0]
    block_refs = refs[1 : 1 + n_blocks]
    alpha_ref, log_ref = refs[1 + n_blocks :]
    seqs, cols = alpha_ref.shape[0], block_refs[0].shape[1]
    total = tree_sum([b[seqs:] for b in block_refs])
    log_ref[...] = jnp.log(total[0, :seqs])
    scale = (states / jnp.broadcast_to(total[0:1], (cols, cols)).T)[:seqs]
    for k in range(n_blocks):
        start = pl.multiple_of((place_ref[0] ^ (0, 3, 2, 1)[k]) * cols, cols)
        alpha_ref[:, pl.ds(start, cols)] = block_refs[k][:seqs] * scale


def hop(x, axis, count, k):
    return lax.ppermute(x, axis, [(i, i ^ k) for i in range(count)])


def swap(x, axis, count):
    return [x] + [hop(x, axis, count, k) for k in (3, 2, 1)]


def on_device(alpha_prev, tokens, src_emb, dst_emb, emission):
    rows = lax.axis_size("row")
    cols = lax.axis_size("col")
    seqs, sources = alpha_prev.shape
    depth, group = dst_emb.shape
    f32 = jnp.float32

    packed = pl.pallas_call(
        pick_rows,
        out_shape=jax.ShapeDtypeStruct((depth + seqs, group), jnp.bfloat16),
        in_specs=[pl.BlockSpec(memory_space=HBM)] * 3,
        out_specs=pl.BlockSpec(memory_space=VMEM),
        scratch_shapes=[
            pltpu.SMEM((seqs,), jnp.int32),
            pltpu.VMEM((seqs * CHUNK, group), jnp.bfloat16),
            pltpu.VMEM((seqs, group), f32),
            pltpu.SemaphoreType.DMA,
            pltpu.SemaphoreType.DMA,
            pltpu.SemaphoreType.DMA,
        ],
        name="pick_rows",
        compiler_params=room(8),
    )(*[pltpu.with_memory_space_constraint(x, HBM) for x in (tokens, emission, dst_emb)])

    paired = rows == 8
    if paired:
        half = rows // 2
        srcs = [src_emb, hop(src_emb, "row", rows, 1)]
        alphas = [alpha_prev, hop(alpha_prev, "row", rows, 1)]
        ready = lax.optimization_barrier((packed, srcs[1]))
        srcs[1] = ready[1]
        like = [packed] + [hop(ready[0], "row", rows, 2 * m) for m in range(1, half)]
        pile = pl.pallas_call(
            stack,
            out_shape=jax.ShapeDtypeStruct((half,) + packed.shape, packed.dtype),
            in_specs=[pl.BlockSpec(memory_space=VMEM)] * half,
            out_specs=pl.BlockSpec(memory_space=VMEM),
            name="stack",
            compiler_params=room(8),
        )(*like)
        arrived = [like, [hop(pile, "row", rows, 1)]]
        sums_shape = (jax.ShapeDtypeStruct((seqs + TAIL, group), f32),) * half
        sums_block = [((seqs + TAIL, group), False)] * half
    else:
        srcs, alphas = [src_emb], [alpha_prev]
        arrived = [[lax.all_gather(packed, "row", axis=0)]]
        sums_shape = (jax.ShapeDtypeStruct((rows, seqs + TAIL, group), f32),)
        sums_block = [((rows, seqs + TAIL, group), False)]

    halves, tiles = len(srcs), len(arrived)
    wide = halves * sources
    tile_rows = rows // tiles
    per_step = math.gcd(tile_rows, 8)
    steps = tile_rows // per_step
    grid = (steps,) if steps > 1 else ()
    dst_block = ((per_step, depth + seqs, group), True)
    expo_block = ((per_step, group, wide), True)
    peak_block = ((tile_rows, wide), False)
    stat_block = ((2, wide), False)
    expos, peaks, stats = [], [], []
    for blocks in arrived:
        expo, peak, stat = pl.pallas_call(
            functools.partial(softmax_tile, steps, per_step, halves, len(blocks)),
            out_shape=(
                jax.ShapeDtypeStruct((tile_rows, group, wide), jnp.bfloat16),
                jax.ShapeDtypeStruct((tile_rows, wide), f32),
                jax.ShapeDtypeStruct((2, wide), f32),
            ),
            grid=grid,
            in_specs=block_specs(
                steps,
                [((sources, depth), False)] * halves + [dst_block] * len(blocks) + [stat_block] * len(stats),
            ),
            out_specs=block_specs(steps, [expo_block, peak_block, stat_block]),
            name="softmax_tile",
            compiler_params=room(16),
        )(*srcs, *blocks, *stats)
        expos.append(expo)
        peaks.append(peak)
        stats = [stat]

    flat = sum(arrived, [])
    partial = pl.pallas_call(
        functools.partial(carry_tile, steps, per_step * tiles, cols, halves, tiles, len(sums_shape)),
        out_shape=sums_shape,
        grid=grid,
        in_specs=block_specs(
            steps,
            [stat_block] * cols
            + [((seqs, sources), False)] * halves
            + [expo_block] * tiles
            + [peak_block] * tiles
            + [dst_block] * len(flat),
        ),
        out_specs=block_specs(steps, sums_block),
        scratch_shapes=[pltpu.VMEM((group, group), f32)],
        name="carry_tile",
        compiler_params=room(16),
    )(*swap(stats[0], "col", cols), *alphas, *expos, *peaks, *flat)

    if paired:
        parts = [partial[0]] + [hop(partial[m], "row", rows, 2 * m) for m in range(1, half)]
    else:
        parts = [lax.all_to_all(partial[0], "row", 0, 0)]
    block = pl.pallas_call(
        emit_block,
        out_shape=jax.ShapeDtypeStruct((seqs + TAIL, group), f32),
        in_specs=[pl.BlockSpec(memory_space=VMEM)] * (1 + len(parts)),
        out_specs=pl.BlockSpec(memory_space=VMEM),
        name="emit_block",
        compiler_params=room(8),
    )(packed, *parts)

    blocks = swap(block, "col", cols)
    place = lax.axis_index("col").astype(jnp.int32).reshape(1)
    return pl.pallas_call(
        functools.partial(finish, float(group * rows * cols), cols),
        out_shape=(jax.ShapeDtypeStruct((seqs, group * cols), f32), jax.ShapeDtypeStruct((seqs,), f32)),
        in_specs=[pl.BlockSpec(memory_space=SMEM)] + [pl.BlockSpec(memory_space=VMEM)] * cols,
        out_specs=(pl.BlockSpec(memory_space=VMEM), pl.BlockSpec(memory_space=VMEM)),
        name="finish",
        compiler_params=room(8),
    )(place, *blocks)


def solution(mesh):
    placed = (P(None, "row"), P(), P("row", None), P(None, ("row", "col")), P(None, ("row", "col")))
    return jax.shard_map(
        on_device, mesh=mesh, in_specs=placed, out_specs=(P(None, "row"), P()), check_vma=False
    )
```

```python
import functools
import math

import jax
import jax.numpy as jnp
from jax import lax
from jax.experimental import pallas as pl
from jax.experimental.pallas import tpu as pltpu
from jax.sharding import PartitionSpec as P

VMEM = pltpu.MemorySpace.VMEM
SMEM = pltpu.MemorySpace.SMEM
HBM = pltpu.MemorySpace.HBM
TAIL = 8
JOINT = 2
CHUNK = 8


def room(mebibytes):
    return pltpu.CompilerParams(vmem_limit_bytes=mebibytes << 20)


def block_specs(steps, shapes):
    if steps == 1:
        return [pl.BlockSpec(memory_space=VMEM) for _ in shapes]
    return [
        pl.BlockSpec(shape, lambda s, n=len(shape), moves=moves: (s if moves else 0,) + (0,) * (n - 1))
        for shape, moves in shapes
    ]


def pick_rows(tokens_ref, table_ref, dst_ref, out_ref, ids, chunks, picked, ids_sem, dst_sem, sem):
    seqs = picked.shape[0]
    depth = dst_ref.shape[0]
    ids_copy = pltpu.make_async_copy(tokens_ref, ids, ids_sem)
    dst_copy = pltpu.make_async_copy(dst_ref, out_ref.at[pl.ds(0, depth)], dst_sem)
    ids_copy.start()
    dst_copy.start()
    ids_copy.wait()
    for b in range(seqs):
        first = pl.multiple_of((ids[b] // CHUNK) * CHUNK, CHUNK)
        pltpu.make_async_copy(
            table_ref.at[pl.ds(first, CHUNK)], chunks.at[pl.ds(b * CHUNK, CHUNK)], sem
        ).start()
    pltpu.make_async_copy(table_ref.at[pl.ds(0, seqs * CHUNK)], chunks, sem).wait()
    rows = lax.broadcasted_iota(jnp.int32, (CHUNK, chunks.shape[1]), 0)
    for b in range(seqs):
        chunk = chunks[b * CHUNK : (b + 1) * CHUNK].astype(jnp.float32)
        kept = jnp.where(rows == ids[b] % CHUNK, chunk, 0.0)
        picked[b : b + 1] = jnp.sum(kept, axis=0, keepdims=True)
    out_ref[depth:] = picked[...].astype(out_ref.dtype)
    dst_copy.wait()


def merge(first, second):
    peak = jnp.maximum(first[0], second[0])
    return peak, first[1] * jnp.exp(first[0] - peak) + second[1] * jnp.exp(second[0] - peak)


def softmax_tile(steps, per_step, n_src, n_dst, *refs):
    src_refs, dst_refs = refs[:n_src], pieces(refs[n_src : n_src + n_dst])
    earlier = refs[n_src + n_dst : -3]
    expo_ref, peak_ref, stat_ref = refs[-3:]
    step = pl.program_id(0) if steps > 1 else 0
    depth = src_refs[0].shape[1]
    for h, src_ref in enumerate(src_refs):
        lanes = slice(h * src_ref.shape[0], (h + 1) * src_ref.shape[0])
        stats = []
        width = dst_refs[0].shape[1]
        for first in range(0, per_step, JOINT):
            some = range(first, min(first + JOINT, per_step))
            columns = jnp.concatenate([dst_refs[q][:depth] for q in some], axis=1)
            tall = lax.dot_general(
                columns, src_ref[...], (((0,), (1,)), ((), ())), preferred_element_type=jnp.float32
            )
            for q in some:
                logits = tall[(q - first) * width : (q - first + 1) * width]
                peak = jnp.max(logits, axis=0, keepdims=True)
                shifted = jnp.exp(logits - peak)
                peak_ref[pl.ds(step * per_step + q, 1), lanes] = peak
                stats.append((peak, jnp.sum(shifted, axis=0, keepdims=True)))
                expo_ref[q, :, lanes] = shifted.astype(expo_ref.dtype)
        local_peak = functools.reduce(jnp.maximum, [p for p, _ in stats])
        local_total = functools.reduce(jnp.add, [t * jnp.exp(p - local_peak) for p, t in stats])

        def put(pair, lanes=lanes):
            stat_ref[0:1, lanes], stat_ref[1:2, lanes] = pair

        if earlier:
            put(merge((local_peak, local_total), (earlier[0][0:1, lanes], earlier[0][1:2, lanes])))
        elif steps == 1:
            put((local_peak, local_total))
        else:

            @pl.when(step == 0)
            def _(put=put, pair=(local_peak, local_total)):
                put(pair)

            @pl.when(step > 0)
            def _(put=put, pair=(local_peak, local_total), lanes=lanes):
                put(merge((stat_ref[0:1, lanes], stat_ref[1:2, lanes]), pair))


def carry_tile(steps, per_step, n_stats, n_src, n_tiles, n_out, *refs):
    if n_out > 1:
        core_ref, refs = refs[0], refs[1:]
    stat_refs, refs = refs[:n_stats], refs[n_stats:]
    alpha_refs, refs = refs[:n_src], refs[n_src:]
    expo_refs, refs = refs[:n_tiles], refs[n_tiles:]
    peak_refs, refs = refs[:n_tiles], refs[n_tiles:]
    emit_refs, out_refs, spread = pieces(refs[: -1 - n_out]), refs[-1 - n_out : -1], refs[-1]
    step = pl.program_id(0) if steps > 1 else 0
    seqs, sources = alpha_refs[0].shape
    each = per_step // n_tiles

    @pl.when(step == 0)
    def _():
        spread[...] = jnp.zeros_like(spread)

    scales = []
    for h in range(n_src):
        lanes = slice(h * sources, (h + 1) * sources)
        turned = slice((n_src - 1 - h) * sources, (n_src - h) * sources)
        known = [(s[0:1, at], s[1:2, at]) for s, at in zip(stat_refs, [lanes] * (n_stats - 1) + [turned], strict=True)]
        row_peak = functools.reduce(jnp.maximum, [p for p, _ in known])
        scales.append((lanes, row_peak, tree_sum([t * jnp.exp(p - row_peak) for p, t in known])))
    shares = []
    for t in range(n_tiles):
        terms = []
        for i in range(each):
            slot = step * each + i
            product = []
            for alpha_ref, (lanes, row_peak, row_total) in zip(alpha_refs, scales, strict=True):
                row_scale = jnp.exp(peak_refs[t][pl.ds(slot, 1), lanes] - row_peak) / row_total
                weights = (alpha_ref[...] * row_scale).astype(jnp.bfloat16)
                product.append(
                    lax.dot_general(
                        weights,
                        expo_refs[t][i, :, lanes],
                        (((1,), (1,)), ((), ())),
                        preferred_element_type=jnp.float32,
                    )
                )
            product = tree_sum(product)
            if n_out == 1:
                out_refs[0][slot, :seqs] = product
            elif i in (0, 3):
                out_refs[i // 3][t, :seqs] = product
            elif i == 1:
                beside = product
            else:
                out_refs[2][t, :seqs] = jnp.where(core_ref[0] == 0, beside, product)
            emit_ref = emit_refs[t * each + i]
            terms.append(product * emit_ref[emit_ref.shape[0] - seqs :].astype(jnp.float32))
        shares.append(functools.reduce(jnp.add, terms))
    spread[:seqs] += tree_sum(shares)

    @pl.when(step == steps - 1)
    def _():
        share = jnp.sum(spread[...].T, axis=0, keepdims=True)
        tail = jnp.broadcast_to(share, (TAIL, share.shape[1]))
        for out_ref in out_refs:
            for group in range(out_ref.shape[0]):
                out_ref[group, seqs:] = tail


def pieces(refs):
    views = [[r.at[i] for i in range(r.shape[0])] if len(r.shape) == 3 else [r] for r in refs]
    return sum(views, [])


def stack(*refs):
    for i, ref in enumerate(refs[:-1]):
        refs[-1][i] = ref[...]


def tree_sum(terms):
    while len(terms) > 1:
        terms = [a + b for a, b in zip(terms[::2], terms[1::2], strict=True)]
    return terms[0]


def emit_block(parts_ref, own_ref, out_ref):
    seqs = out_ref.shape[0] - TAIL
    sums = jnp.sum(parts_ref[...], axis=0)
    out_ref[:seqs] = sums[:seqs] * own_ref[own_ref.shape[0] - seqs :].astype(jnp.float32)
    out_ref[seqs:] = sums[seqs:]


def emit_pair(own_ref, corner_ref, asked_ref, told_ref, mine_ref, theirs_ref, out_ref):
    seqs = out_ref.shape[1] - TAIL
    for t, emit_ref in enumerate((mine_ref, theirs_ref.at[0])):
        sums = (own_ref[t] + corner_ref[t]) + (asked_ref[t] + told_ref[1 - t])
        out_ref[t, :seqs] = sums[:seqs] * emit_ref[emit_ref.shape[0] - seqs :].astype(jnp.float32)
        out_ref[t, seqs:] = sums[seqs:]


def finish(states, n_blocks, *refs):
    place_refs, block_refs = refs[:n_blocks], refs[n_blocks : 2 * n_blocks]
    alpha_ref, log_ref = refs[2 * n_blocks :]
    seqs, cols = alpha_ref.shape[0], block_refs[0].shape[-1]
    views = [b if len(b.shape) == 2 else b.at[k // 3] for k, b in enumerate(block_refs)]
    total = tree_sum([b[seqs:] for b in views])
    log_ref[...] = jnp.log(total[0, :seqs])
    scale = (states / jnp.broadcast_to(total[0:1], (cols, cols)).T)[:seqs]
    for place_ref, block in zip(place_refs, views, strict=True):
        start = pl.multiple_of(place_ref[0] * cols, cols)
        alpha_ref[:, pl.ds(start, cols)] = block[:seqs] * scale


def hop(x, axis, count, k):
    return lax.ppermute(x, axis, [(i, i ^ k) for i in range(count)])


def exchange(x, rows, cols, paired):
    here = lax.axis_index("col").astype(jnp.int32)
    if not paired:
        turns = [0] + list(range(cols - 1, 0, -1))
        return [x] + [hop(x, "col", cols, k) for k in turns[1:]], [here ^ k for k in turns]
    odd = lax.axis_index("row").astype(jnp.int32) & 1
    mixed = [(r * cols + c, r * cols + (c ^ (3 if r % 2 else 1))) for r in range(rows) for c in range(cols)]
    asked = lax.ppermute(x, ("row", "col"), mixed)
    arrays = [x, hop(x, "col", cols, 2), asked, hop(asked, "row", rows, 1)]
    return arrays, [here, here ^ 2, here ^ (1 + 2 * odd), here ^ (3 - 2 * odd)]


def on_device(alpha_prev, tokens, src_emb, dst_emb, emission):
    rows = lax.axis_size("row")
    cols = lax.axis_size("col")
    seqs, sources = alpha_prev.shape
    depth, group = dst_emb.shape
    f32 = jnp.float32

    packed = pl.pallas_call(
        pick_rows,
        out_shape=jax.ShapeDtypeStruct((depth + seqs, group), jnp.bfloat16),
        in_specs=[pl.BlockSpec(memory_space=HBM)] * 3,
        out_specs=pl.BlockSpec(memory_space=VMEM),
        scratch_shapes=[
            pltpu.SMEM((seqs,), jnp.int32),
            pltpu.VMEM((seqs * CHUNK, group), jnp.bfloat16),
            pltpu.VMEM((seqs, group), f32),
            pltpu.SemaphoreType.DMA,
            pltpu.SemaphoreType.DMA,
            pltpu.SemaphoreType.DMA,
        ],
        name="pick_rows",
        compiler_params=room(8),
    )(*[pltpu.with_memory_space_constraint(x, HBM) for x in (tokens, emission, dst_emb)])

    paired = rows == 8 and cols == 4
    if paired:
        half = rows // 2
        srcs = [src_emb, hop(src_emb, "row", rows, 1)]
        alphas = [alpha_prev, hop(alpha_prev, "row", rows, 1)]
        ready = lax.optimization_barrier((packed, srcs[1]))
        srcs[1] = ready[1]
        like = [packed] + [hop(ready[0], "row", rows, 2 * m) for m in range(1, half)]
        pile = pl.pallas_call(
            stack,
            out_shape=jax.ShapeDtypeStruct((half,) + packed.shape, packed.dtype),
            in_specs=[pl.BlockSpec(memory_space=VMEM)] * half,
            out_specs=pl.BlockSpec(memory_space=VMEM),
            name="stack",
            compiler_params=room(8),
        )(*like)
        arrived = [like, [hop(pile, "row", rows, 1)]]
        core = (lax.axis_index("row").astype(jnp.int32) & 1).reshape(1)
        sums_shape = (jax.ShapeDtypeStruct((2, seqs + TAIL, group), f32),) * 3
        sums_block = [((2, seqs + TAIL, group), False)] * 3
    else:
        srcs, alphas = [src_emb], [alpha_prev]
        arrived = [[lax.all_gather(packed, "row", axis=0)]]
        sums_shape = (jax.ShapeDtypeStruct((rows, seqs + TAIL, group), f32),)
        sums_block = [((rows, seqs + TAIL, group), False)]

    halves, tiles = len(srcs), len(arrived)
    wide = halves * sources
    tile_rows = rows // tiles
    per_step = math.gcd(tile_rows, 8)
    steps = tile_rows // per_step
    grid = (steps,) if steps > 1 else ()
    dst_block = ((per_step, depth + seqs, group), True)
    expo_block = ((per_step, group, wide), True)
    peak_block = ((tile_rows, wide), False)
    stat_block = ((2, wide), False)
    expos, peaks, stats = [], [], []
    for blocks in arrived:
        expo, peak, stat = pl.pallas_call(
            functools.partial(softmax_tile, steps, per_step, halves, len(blocks)),
            out_shape=(
                jax.ShapeDtypeStruct((tile_rows, group, wide), jnp.bfloat16),
                jax.ShapeDtypeStruct((tile_rows, wide), f32),
                jax.ShapeDtypeStruct((2, wide), f32),
            ),
            grid=grid,
            in_specs=block_specs(
                steps,
                [((sources, depth), False)] * halves + [dst_block] * len(blocks) + [stat_block] * len(stats),
            ),
            out_specs=block_specs(steps, [expo_block, peak_block, stat_block]),
            name="softmax_tile",
            compiler_params=room(16),
        )(*srcs, *blocks, *stats)
        expos.append(expo)
        peaks.append(peak)
        stats = [stat]

    known, _ = exchange(stats[0], rows, cols, paired)
    flat = sum(arrived, [])
    partial = pl.pallas_call(
        functools.partial(carry_tile, steps, per_step * tiles, cols, halves, tiles, len(sums_shape)),
        out_shape=sums_shape,
        grid=grid,
        in_specs=[pl.BlockSpec(memory_space=SMEM)] * paired
        + block_specs(
            steps,
            [stat_block] * cols
            + [((seqs, sources), False)] * halves
            + [expo_block] * tiles
            + [peak_block] * tiles
            + [dst_block] * len(flat),
        ),
        out_specs=block_specs(steps, sums_block),
        scratch_shapes=[pltpu.VMEM((group, group), f32)],
        name="carry_tile",
        compiler_params=room(16),
    )(*([core] if paired else []), *known, *alphas, *expos, *peaks, *flat)

    if paired:
        own, corner, turned = partial
        asked = lax.ppermute(turned, "row", [(i, i ^ (4 if i % 2 else 2)) for i in range(rows)])
        corner = hop(corner, "row", rows, rows - 2)
        told = hop(asked, "row", rows, 1)
        body, operands = emit_pair, (own, corner, asked, told, packed, arrived[1][0])
        block_shape = (2, seqs + TAIL, group)
    else:
        body, operands = emit_block, (lax.all_to_all(partial[0], "row", 0, 0), packed)
        block_shape = (seqs + TAIL, group)
    block = pl.pallas_call(
        body,
        out_shape=jax.ShapeDtypeStruct(block_shape, f32),
        in_specs=[pl.BlockSpec(memory_space=VMEM)] * len(operands),
        out_specs=pl.BlockSpec(memory_space=VMEM),
        name="emit_block",
        compiler_params=room(8),
    )(*operands)

    blocks, places = exchange(block, rows, cols, paired)
    return pl.pallas_call(
        functools.partial(finish, float(group * rows * cols), cols),
        out_shape=(jax.ShapeDtypeStruct((seqs, group * cols), f32), jax.ShapeDtypeStruct((seqs,), f32)),
        in_specs=[pl.BlockSpec(memory_space=SMEM)] * cols + [pl.BlockSpec(memory_space=VMEM)] * cols,
        out_specs=(pl.BlockSpec(memory_space=VMEM), pl.BlockSpec(memory_space=VMEM)),
        name="finish",
        compiler_params=room(8),
    )(*[p.reshape(1) for p in places], *blocks)


def solution(mesh):
    placed = (P(None, "row"), P(), P("row", None), P(None, ("row", "col")), P(None, ("row", "col")))
    return jax.shard_map(
        on_device, mesh=mesh, in_specs=placed, out_specs=(P(None, "row"), P()), check_vma=False
    )
```

```python
import functools
import math

import jax
import jax.numpy as jnp
from jax import lax
from jax.experimental import pallas as pl
from jax.experimental.pallas import tpu as pltpu
from jax.sharding import PartitionSpec as P

VMEM = pltpu.MemorySpace.VMEM
SMEM = pltpu.MemorySpace.SMEM
HBM = pltpu.MemorySpace.HBM
TAIL = 8
JOINT = 2
CHUNK = 8


def room(mebibytes):
    return pltpu.CompilerParams(vmem_limit_bytes=mebibytes << 20)


def block_specs(steps, shapes):
    if steps == 1:
        return [pl.BlockSpec(memory_space=VMEM) for _ in shapes]
    return [
        pl.BlockSpec(shape, lambda s, n=len(shape), moves=moves: (s if moves else 0,) + (0,) * (n - 1))
        for shape, moves in shapes
    ]


def pick_rows(tokens_ref, table_ref, dst_ref, out_ref, ids, chunks, picked, ids_sem, dst_sem, sem):
    seqs = picked.shape[0]
    depth = dst_ref.shape[0]
    ids_copy = pltpu.make_async_copy(tokens_ref, ids, ids_sem)
    dst_copy = pltpu.make_async_copy(dst_ref, out_ref.at[pl.ds(0, depth)], dst_sem)
    ids_copy.start()
    dst_copy.start()
    ids_copy.wait()
    for b in range(seqs):
        first = pl.multiple_of((ids[b] // CHUNK) * CHUNK, CHUNK)
        pltpu.make_async_copy(
            table_ref.at[pl.ds(first, CHUNK)], chunks.at[pl.ds(b * CHUNK, CHUNK)], sem
        ).start()
    pltpu.make_async_copy(table_ref.at[pl.ds(0, seqs * CHUNK)], chunks, sem).wait()
    rows = lax.broadcasted_iota(jnp.int32, (CHUNK, chunks.shape[1]), 0)
    for b in range(seqs):
        chunk = chunks[b * CHUNK : (b + 1) * CHUNK].astype(jnp.float32)
        kept = jnp.where(rows == ids[b] % CHUNK, chunk, 0.0)
        picked[b : b + 1] = jnp.sum(kept, axis=0, keepdims=True)
    out_ref[depth:] = picked[...].astype(out_ref.dtype)
    dst_copy.wait()


def merge(first, second):
    peak = jnp.maximum(first[0], second[0])
    return peak, first[1] * jnp.exp(first[0] - peak) + second[1] * jnp.exp(second[0] - peak)


def softmax_tile(steps, per_step, n_src, n_dst, *refs):
    src_refs, dst_refs = refs[:n_src], pieces(refs[n_src : n_src + n_dst])
    earlier = refs[n_src + n_dst : -3]
    expo_ref, peak_ref, stat_ref = refs[-3:]
    step = pl.program_id(0) if steps > 1 else 0
    depth = src_refs[0].shape[1]
    for h, src_ref in enumerate(src_refs):
        lanes = slice(h * src_ref.shape[0], (h + 1) * src_ref.shape[0])
        stats = []
        width = dst_refs[0].shape[1]
        for first in range(0, per_step, JOINT):
            some = range(first, min(first + JOINT, per_step))
            columns = jnp.concatenate([dst_refs[q][:depth] for q in some], axis=1)
            tall = lax.dot_general(
                columns, src_ref[...], (((0,), (1,)), ((), ())), preferred_element_type=jnp.float32
            )
            for q in some:
                logits = tall[(q - first) * width : (q - first + 1) * width]
                peak = jnp.max(logits, axis=0, keepdims=True)
                shifted = jnp.exp(logits - peak)
                peak_ref[pl.ds(step * per_step + q, 1), lanes] = peak
                stats.append((peak, jnp.sum(shifted, axis=0, keepdims=True)))
                expo_ref[q, :, lanes] = shifted.astype(expo_ref.dtype)
        local_peak = functools.reduce(jnp.maximum, [p for p, _ in stats])
        local_total = functools.reduce(jnp.add, [t * jnp.exp(p - local_peak) for p, t in stats])

        def put(pair, lanes=lanes):
            stat_ref[0:1, lanes], stat_ref[1:2, lanes] = pair

        if earlier:
            put(merge((local_peak, local_total), (earlier[0][0:1, lanes], earlier[0][1:2, lanes])))
        elif steps == 1:
            put((local_peak, local_total))
        else:

            @pl.when(step == 0)
            def _(put=put, pair=(local_peak, local_total)):
                put(pair)

            @pl.when(step > 0)
            def _(put=put, pair=(local_peak, local_total), lanes=lanes):
                put(merge((stat_ref[0:1, lanes], stat_ref[1:2, lanes]), pair))


def carry_tile(steps, per_step, n_stats, n_src, n_tiles, n_out, *refs):
    stat_refs, refs = refs[:n_stats], refs[n_stats:]
    alpha_refs, refs = refs[:n_src], refs[n_src:]
    expo_refs, refs = refs[:n_tiles], refs[n_tiles:]
    peak_refs, refs = refs[:n_tiles], refs[n_tiles:]
    emit_refs, out_refs, spread = pieces(refs[: -1 - n_out]), refs[-1 - n_out : -1], refs[-1]
    step = pl.program_id(0) if steps > 1 else 0
    seqs, sources = alpha_refs[0].shape
    each = per_step // n_tiles

    @pl.when(step == 0)
    def _():
        spread[...] = jnp.zeros_like(spread)

    scales = []
    for h in range(n_src):
        lanes = slice(h * sources, (h + 1) * sources)
        turned = slice((n_src - 1 - h) * sources, (n_src - h) * sources)
        known = [(s[0:1, at], s[1:2, at]) for s, at in zip(stat_refs, [lanes] * (n_stats - 1) + [turned], strict=True)]
        row_peak = functools.reduce(jnp.maximum, [p for p, _ in known])
        scales.append((lanes, row_peak, tree_sum([t * jnp.exp(p - row_peak) for p, t in known])))
    shares = []
    for t in range(n_tiles):
        terms = []
        for i in range(each):
            slot = step * each + i
            product = []
            for alpha_ref, (lanes, row_peak, row_total) in zip(alpha_refs, scales, strict=True):
                row_scale = jnp.exp(peak_refs[t][pl.ds(slot, 1), lanes] - row_peak) / row_total
                weights = (alpha_ref[...] * row_scale).astype(jnp.bfloat16)
                product.append(
                    lax.dot_general(
                        weights,
                        expo_refs[t][i, :, lanes],
                        (((1,), (1,)), ((), ())),
                        preferred_element_type=jnp.float32,
                    )
                )
            product = tree_sum(product)
            if n_out == 1:
                out_refs[0][slot, :seqs] = product
            elif i in (0, 3):
                out_refs[i // 3][t, :seqs] = product
            elif i == 1 + t:
                out_refs[2][t, :seqs] = product
            emit_ref = emit_refs[t * each + i]
            terms.append(product * emit_ref[emit_ref.shape[0] - seqs :].astype(jnp.float32))
        shares.append(functools.reduce(jnp.add, terms))
    spread[:seqs] += tree_sum(shares)

    @pl.when(step == steps - 1)
    def _():
        share = jnp.sum(spread[...].T, axis=0, keepdims=True)
        tail = jnp.broadcast_to(share, (TAIL, share.shape[1]))
        for out_ref in out_refs:
            for group in range(out_ref.shape[0]):
                out_ref[group, seqs:] = tail


def pieces(refs):
    views = [[r.at[i] for i in range(r.shape[0])] if len(r.shape) == 3 else [r] for r in refs]
    return sum(views, [])


def stack(*refs):
    for i, ref in enumerate(refs[:-1]):
        refs[-1][i] = ref[...]


def tree_sum(terms):
    while len(terms) > 1:
        terms = [a + b for a, b in zip(terms[::2], terms[1::2], strict=True)]
    return terms[0]


def emit_block(parts_ref, own_ref, out_ref):
    seqs = out_ref.shape[0] - TAIL
    sums = jnp.sum(parts_ref[...], axis=0)
    out_ref[:seqs] = sums[:seqs] * own_ref[own_ref.shape[0] - seqs :].astype(jnp.float32)
    out_ref[seqs:] = sums[seqs:]


def emit_pair(own_ref, corner_ref, asked_ref, told_ref, mine_ref, theirs_ref, out_ref):
    seqs = out_ref.shape[1] - TAIL
    for t, emit_ref in enumerate((mine_ref, theirs_ref.at[0])):
        sums = (own_ref[t] + corner_ref[t]) + (asked_ref[t] + told_ref[1 - t])
        out_ref[t, :seqs] = sums[:seqs] * emit_ref[emit_ref.shape[0] - seqs :].astype(jnp.float32)
        out_ref[t, seqs:] = sums[seqs:]


def finish(states, n_blocks, *refs):
    place_refs, block_refs = refs[:n_blocks], refs[n_blocks : 2 * n_blocks]
    alpha_ref, log_ref = refs[2 * n_blocks :]
    seqs, cols = alpha_ref.shape[0], block_refs[0].shape[-1]
    views = [b if len(b.shape) == 2 else b.at[k // 3] for k, b in enumerate(block_refs)]
    total = tree_sum([b[seqs:] for b in views])
    log_ref[...] = jnp.log(total[0, :seqs])
    scale = (states / jnp.broadcast_to(total[0:1], (cols, cols)).T)[:seqs]
    for place_ref, block in zip(place_refs, views, strict=True):
        start = pl.multiple_of(place_ref[0] * cols, cols)
        alpha_ref[:, pl.ds(start, cols)] = block[:seqs] * scale


def ask(x, count, even, odd):
    return lax.ppermute(x, "row", [(i, i ^ (odd if i % 2 else even)) for i in range(count)])


def hop(x, axis, count, k):
    return lax.ppermute(x, axis, [(i, i ^ k) for i in range(count)])


def exchange(x, rows, cols, paired):
    here = lax.axis_index("col").astype(jnp.int32)
    if not paired:
        turns = [0] + list(range(cols - 1, 0, -1))
        return [x] + [hop(x, "col", cols, k) for k in turns[1:]], [here ^ k for k in turns]
    odd = lax.axis_index("row").astype(jnp.int32) & 1
    mixed = [(r * cols + c, r * cols + (c ^ (3 if r % 2 else 1))) for r in range(rows) for c in range(cols)]
    asked = lax.ppermute(x, ("row", "col"), mixed)
    arrays = [x, hop(x, "col", cols, 2), asked, hop(asked, "row", rows, 1)]
    return arrays, [here, here ^ 2, here ^ (1 + 2 * odd), here ^ (3 - 2 * odd)]


def on_device(alpha_prev, tokens, src_emb, dst_emb, emission):
    rows = lax.axis_size("row")
    cols = lax.axis_size("col")
    seqs, sources = alpha_prev.shape
    depth, group = dst_emb.shape
    f32 = jnp.float32

    packed = pl.pallas_call(
        pick_rows,
        out_shape=jax.ShapeDtypeStruct((depth + seqs, group), jnp.bfloat16),
        in_specs=[pl.BlockSpec(memory_space=HBM)] * 3,
        out_specs=pl.BlockSpec(memory_space=VMEM),
        scratch_shapes=[
            pltpu.SMEM((seqs,), jnp.int32),
            pltpu.VMEM((seqs * CHUNK, group), jnp.bfloat16),
            pltpu.VMEM((seqs, group), f32),
            pltpu.SemaphoreType.DMA,
            pltpu.SemaphoreType.DMA,
            pltpu.SemaphoreType.DMA,
        ],
        name="pick_rows",
        compiler_params=room(8),
    )(*[pltpu.with_memory_space_constraint(x, HBM) for x in (tokens, emission, dst_emb)])

    paired = rows == 8 and cols == 4
    if paired:
        half = rows // 2
        srcs = [src_emb, hop(src_emb, "row", rows, 1)]
        alphas = [alpha_prev, hop(alpha_prev, "row", rows, 1)]
        ready = lax.optimization_barrier((packed, srcs[1]))
        srcs[1] = ready[1]
        like = [packed, ask(ready[0], rows, 2, 4), ask(ready[0], rows, 4, 2), hop(ready[0], "row", rows, rows - 2)]
        pile = pl.pallas_call(
            stack,
            out_shape=jax.ShapeDtypeStruct((half,) + packed.shape, packed.dtype),
            in_specs=[pl.BlockSpec(memory_space=VMEM)] * half,
            out_specs=pl.BlockSpec(memory_space=VMEM),
            name="stack",
            compiler_params=room(8),
        )(*like)
        arrived = [like, [hop(pile, "row", rows, 1)]]
        sums_shape = (jax.ShapeDtypeStruct((2, seqs + TAIL, group), f32),) * 3
        sums_block = [((2, seqs + TAIL, group), False)] * 3
    else:
        srcs, alphas = [src_emb], [alpha_prev]
        arrived = [[lax.all_gather(packed, "row", axis=0)]]
        sums_shape = (jax.ShapeDtypeStruct((rows, seqs + TAIL, group), f32),)
        sums_block = [((rows, seqs + TAIL, group), False)]

    halves, tiles = len(srcs), len(arrived)
    wide = halves * sources
    tile_rows = rows // tiles
    per_step = math.gcd(tile_rows, 8)
    steps = tile_rows // per_step
    grid = (steps,) if steps > 1 else ()
    dst_block = ((per_step, depth + seqs, group), True)
    expo_block = ((per_step, group, wide), True)
    peak_block = ((tile_rows, wide), False)
    stat_block = ((2, wide), False)
    expos, peaks, stats = [], [], []
    for blocks in arrived:
        expo, peak, stat = pl.pallas_call(
            functools.partial(softmax_tile, steps, per_step, halves, len(blocks)),
            out_shape=(
                jax.ShapeDtypeStruct((tile_rows, group, wide), jnp.bfloat16),
                jax.ShapeDtypeStruct((tile_rows, wide), f32),
                jax.ShapeDtypeStruct((2, wide), f32),
            ),
            grid=grid,
            in_specs=block_specs(
                steps,
                [((sources, depth), False)] * halves + [dst_block] * len(blocks) + [stat_block] * len(stats),
            ),
            out_specs=block_specs(steps, [expo_block, peak_block, stat_block]),
            name="softmax_tile",
            compiler_params=room(16),
        )(*srcs, *blocks, *stats)
        expos.append(expo)
        peaks.append(peak)
        stats = [stat]

    known, _ = exchange(stats[0], rows, cols, paired)
    flat = sum(arrived, [])
    partial = pl.pallas_call(
        functools.partial(carry_tile, steps, per_step * tiles, cols, halves, tiles, len(sums_shape)),
        out_shape=sums_shape,
        grid=grid,
        in_specs=block_specs(
            steps,
            [stat_block] * cols
            + [((seqs, sources), False)] * halves
            + [expo_block] * tiles
            + [peak_block] * tiles
            + [dst_block] * len(flat),
        ),
        out_specs=block_specs(steps, sums_block),
        scratch_shapes=[pltpu.VMEM((group, group), f32)],
        name="carry_tile",
        compiler_params=room(16),
    )(*known, *alphas, *expos, *peaks, *flat)

    if paired:
        own, corner, turned = partial
        asked = ask(turned, rows, 2, 4)
        corner = hop(corner, "row", rows, rows - 2)
        told = hop(asked, "row", rows, 1)
        body, operands = emit_pair, (own, corner, asked, told, packed, arrived[1][0])
        block_shape = (2, seqs + TAIL, group)
    else:
        body, operands = emit_block, (lax.all_to_all(partial[0], "row", 0, 0), packed)
        block_shape = (seqs + TAIL, group)
    block = pl.pallas_call(
        body,
        out_shape=jax.ShapeDtypeStruct(block_shape, f32),
        in_specs=[pl.BlockSpec(memory_space=VMEM)] * len(operands),
        out_specs=pl.BlockSpec(memory_space=VMEM),
        name="emit_block",
        compiler_params=room(8),
    )(*operands)

    blocks, places = exchange(block, rows, cols, paired)
    return pl.pallas_call(
        functools.partial(finish, float(group * rows * cols), cols),
        out_shape=(jax.ShapeDtypeStruct((seqs, group * cols), f32), jax.ShapeDtypeStruct((seqs,), f32)),
        in_specs=[pl.BlockSpec(memory_space=SMEM)] * cols + [pl.BlockSpec(memory_space=VMEM)] * cols,
        out_specs=(pl.BlockSpec(memory_space=VMEM), pl.BlockSpec(memory_space=VMEM)),
        name="finish",
        compiler_params=room(8),
    )(*[p.reshape(1) for p in places], *blocks)


def solution(mesh):
    placed = (P(None, "row"), P(), P("row", None), P(None, ("row", "col")), P(None, ("row", "col")))
    return jax.shard_map(
        on_device, mesh=mesh, in_specs=placed, out_specs=(P(None, "row"), P()), check_vma=False
    )
```

```python
import functools
import math

import jax
import jax.numpy as jnp
from jax import lax
from jax.experimental import pallas as pl
from jax.experimental.pallas import tpu as pltpu
from jax.sharding import PartitionSpec as P

VMEM = pltpu.MemorySpace.VMEM
SMEM = pltpu.MemorySpace.SMEM
HBM = pltpu.MemorySpace.HBM
TAIL = 8
JOINT = 2
CHUNK = 8


def room(mebibytes):
    return pltpu.CompilerParams(vmem_limit_bytes=mebibytes << 20)


def block_specs(steps, shapes):
    if steps == 1:
        return [pl.BlockSpec(memory_space=VMEM) for _ in shapes]
    return [
        pl.BlockSpec(shape, lambda s, n=len(shape), moves=moves: (s if moves else 0,) + (0,) * (n - 1))
        for shape, moves in shapes
    ]


def pick_rows(tokens_ref, table_ref, dst_ref, out_ref, ids, chunks, picked, ids_sem, dst_sem, sem):
    seqs = picked.shape[0]
    depth = dst_ref.shape[0]
    ids_copy = pltpu.make_async_copy(tokens_ref, ids, ids_sem)
    dst_copy = pltpu.make_async_copy(dst_ref, out_ref.at[pl.ds(0, depth)], dst_sem)
    ids_copy.start()
    dst_copy.start()
    ids_copy.wait()
    for b in range(seqs):
        first = pl.multiple_of((ids[b] // CHUNK) * CHUNK, CHUNK)
        pltpu.make_async_copy(
            table_ref.at[pl.ds(first, CHUNK)], chunks.at[pl.ds(b * CHUNK, CHUNK)], sem
        ).start()
    pltpu.make_async_copy(table_ref.at[pl.ds(0, seqs * CHUNK)], chunks, sem).wait()
    rows = lax.broadcasted_iota(jnp.int32, (CHUNK, chunks.shape[1]), 0)
    for b in range(seqs):
        chunk = chunks[b * CHUNK : (b + 1) * CHUNK].astype(jnp.float32)
        kept = jnp.where(rows == ids[b] % CHUNK, chunk, 0.0)
        picked[b : b + 1] = jnp.sum(kept, axis=0, keepdims=True)
    out_ref[depth:] = picked[...].astype(out_ref.dtype)
    dst_copy.wait()


def merge(first, second):
    peak = jnp.maximum(first[0], second[0])
    return peak, first[1] * jnp.exp(first[0] - peak) + second[1] * jnp.exp(second[0] - peak)


def softmax_tile(steps, per_step, n_src, n_dst, *refs):
    src_refs, dst_refs = refs[:n_src], pieces(refs[n_src : n_src + n_dst])
    earlier = refs[n_src + n_dst : -3]
    expo_ref, peak_ref, stat_ref = refs[-3:]
    step = pl.program_id(0) if steps > 1 else 0
    depth = src_refs[0].shape[1]
    for h, src_ref in enumerate(src_refs):
        lanes = slice(h * src_ref.shape[0], (h + 1) * src_ref.shape[0])
        stats = []
        width = dst_refs[0].shape[1]
        for first in range(0, per_step, JOINT):
            some = range(first, min(first + JOINT, per_step))
            columns = jnp.concatenate([dst_refs[q][:depth] for q in some], axis=1)
            tall = lax.dot_general(
                columns, src_ref[...], (((0,), (1,)), ((), ())), preferred_element_type=jnp.float32
            )
            for q in some:
                logits = tall[(q - first) * width : (q - first + 1) * width]
                peak = jnp.max(logits, axis=0, keepdims=True)
                shifted = jnp.exp(logits - peak)
                peak_ref[pl.ds(step * per_step + q, 1), lanes] = peak
                stats.append((peak, jnp.sum(shifted, axis=0, keepdims=True)))
                expo_ref[q, :, lanes] = shifted.astype(expo_ref.dtype)
        local_peak = functools.reduce(jnp.maximum, [p for p, _ in stats])
        local_total = functools.reduce(jnp.add, [t * jnp.exp(p - local_peak) for p, t in stats])

        def put(pair, lanes=lanes):
            stat_ref[0:1, lanes], stat_ref[1:2, lanes] = pair

        if earlier:
            put(merge((local_peak, local_total), (earlier[0][0:1, lanes], earlier[0][1:2, lanes])))
        elif steps == 1:
            put((local_peak, local_total))
        else:

            @pl.when(step == 0)
            def _(put=put, pair=(local_peak, local_total)):
                put(pair)

            @pl.when(step > 0)
            def _(put=put, pair=(local_peak, local_total), lanes=lanes):
                put(merge((stat_ref[0:1, lanes], stat_ref[1:2, lanes]), pair))


def carry_tile(steps, per_step, n_stats, n_src, n_tiles, n_out, *refs):
    if n_out > 1:
        core_ref, refs = refs[0], refs[1:]
    stat_refs, refs = refs[:n_stats], refs[n_stats:]
    alpha_refs, refs = refs[:n_src], refs[n_src:]
    expo_refs, refs = refs[:n_tiles], refs[n_tiles:]
    peak_refs, refs = refs[:n_tiles], refs[n_tiles:]
    emit_refs, out_refs, spread = pieces(refs[: -1 - n_out]), refs[-1 - n_out : -1], refs[-1]
    step = pl.program_id(0) if steps > 1 else 0
    seqs, sources = alpha_refs[0].shape
    each = per_step // n_tiles

    @pl.when(step == 0)
    def _():
        spread[...] = jnp.zeros_like(spread)

    scales = []
    for h in range(n_src):
        lanes = slice(h * sources, (h + 1) * sources)
        turned = slice((n_src - 1 - h) * sources, (n_src - h) * sources)
        known = [(s[0:1, at], s[1:2, at]) for s, at in zip(stat_refs, [lanes] * (n_stats - 1) + [turned], strict=True)]
        row_peak = functools.reduce(jnp.maximum, [p for p, _ in known])
        share = 1.0 / tree_sum([t * jnp.exp(p - row_peak) for p, t in known])
        rows_at = pl.ds(step * each, each)
        scales.append((lanes, [jnp.exp(p[rows_at, lanes] - row_peak) * share for p in peak_refs]))
    shares = []
    for t in range(n_tiles):
        terms = []
        for i in range(each):
            slot = step * each + i
            product = []
            for alpha_ref, (lanes, row_scales) in zip(alpha_refs, scales, strict=True):
                weights = (alpha_ref[...] * row_scales[t][i : i + 1]).astype(jnp.bfloat16)
                product.append(
                    lax.dot_general(
                        weights,
                        expo_refs[t][i, :, lanes],
                        (((1,), (1,)), ((), ())),
                        preferred_element_type=jnp.float32,
                    )
                )
            product = tree_sum(product)
            if n_out == 1:
                out_refs[0][slot, :seqs] = product
            elif i in (0, 3):
                out_refs[i // 3][t, :seqs] = product
            elif i == 1:
                beside = product
            else:
                out_refs[2][t, :seqs] = jnp.where(core_ref[0] == 0, beside, product)
            emit_ref = emit_refs[t * each + i]
            terms.append(product * emit_ref[emit_ref.shape[0] - seqs :].astype(jnp.float32))
        shares.append(functools.reduce(jnp.add, terms))
    spread[:seqs] += tree_sum(shares)

    @pl.when(step == steps - 1)
    def _():
        share = jnp.sum(spread[...].T, axis=0, keepdims=True)
        tail = jnp.broadcast_to(share, (TAIL, share.shape[1]))
        for out_ref in out_refs:
            for group in range(out_ref.shape[0]):
                out_ref[group, seqs:] = tail


def pieces(refs):
    views = [[r.at[i] for i in range(r.shape[0])] if len(r.shape) == 3 else [r] for r in refs]
    return sum(views, [])


def stack(*refs):
    for i, ref in enumerate(refs[:-1]):
        refs[-1][i] = ref[...]


def tree_sum(terms):
    while len(terms) > 1:
        terms = [a + b for a, b in zip(terms[::2], terms[1::2], strict=True)]
    return terms[0]


def emit_block(parts_ref, own_ref, out_ref):
    seqs = out_ref.shape[0] - TAIL
    sums = jnp.sum(parts_ref[...], axis=0)
    out_ref[:seqs] = sums[:seqs] * own_ref[own_ref.shape[0] - seqs :].astype(jnp.float32)
    out_ref[seqs:] = sums[seqs:]


def emit_pair(own_ref, corner_ref, asked_ref, told_ref, mine_ref, theirs_ref, out_ref):
    seqs = out_ref.shape[1] - TAIL
    for t, emit_ref in enumerate((mine_ref, theirs_ref.at[0])):
        sums = (own_ref[t] + corner_ref[t]) + (asked_ref[t] + told_ref[1 - t])
        out_ref[t, :seqs] = sums[:seqs] * emit_ref[emit_ref.shape[0] - seqs :].astype(jnp.float32)
        out_ref[t, seqs:] = sums[seqs:]


def finish(states, n_blocks, *refs):
    place_refs, block_refs = refs[:n_blocks], refs[n_blocks : 2 * n_blocks]
    alpha_ref, log_ref = refs[2 * n_blocks :]
    seqs, cols = alpha_ref.shape[0], block_refs[0].shape[-1]
    views = [b if len(b.shape) == 2 else b.at[k // 3] for k, b in enumerate(block_refs)]
    total = tree_sum([b[seqs:] for b in views])
    log_ref[...] = jnp.log(total[0, :seqs])
    scale = (states / jnp.broadcast_to(total[0:1], (cols, cols)).T)[:seqs]
    for place_ref, block in zip(place_refs, views, strict=True):
        start = pl.multiple_of(place_ref[0] * cols, cols)
        alpha_ref[:, pl.ds(start, cols)] = block[:seqs] * scale


def hop(x, axis, count, k):
    return lax.ppermute(x, axis, [(i, i ^ k) for i in range(count)])


def exchange(x, rows, cols, paired):
    here = lax.axis_index("col").astype(jnp.int32)
    if not paired:
        turns = [0] + list(range(cols - 1, 0, -1))
        return [x] + [hop(x, "col", cols, k) for k in turns[1:]], [here ^ k for k in turns]
    odd = lax.axis_index("row").astype(jnp.int32) & 1
    mixed = [(r * cols + c, r * cols + (c ^ (3 if r % 2 else 1))) for r in range(rows) for c in range(cols)]
    asked = lax.ppermute(x, ("row", "col"), mixed)
    arrays = [x, hop(x, "col", cols, 2), asked, hop(asked, "row", rows, 1)]
    return arrays, [here, here ^ 2, here ^ (1 + 2 * odd), here ^ (3 - 2 * odd)]


def on_device(alpha_prev, tokens, src_emb, dst_emb, emission):
    rows = lax.axis_size("row")
    cols = lax.axis_size("col")
    seqs, sources = alpha_prev.shape
    depth, group = dst_emb.shape
    f32 = jnp.float32

    packed = pl.pallas_call(
        pick_rows,
        out_shape=jax.ShapeDtypeStruct((depth + seqs, group), jnp.bfloat16),
        in_specs=[pl.BlockSpec(memory_space=HBM)] * 3,
        out_specs=pl.BlockSpec(memory_space=VMEM),
        scratch_shapes=[
            pltpu.SMEM((seqs,), jnp.int32),
            pltpu.VMEM((seqs * CHUNK, group), jnp.bfloat16),
            pltpu.VMEM((seqs, group), f32),
            pltpu.SemaphoreType.DMA,
            pltpu.SemaphoreType.DMA,
            pltpu.SemaphoreType.DMA,
        ],
        name="pick_rows",
        compiler_params=room(8),
    )(*[pltpu.with_memory_space_constraint(x, HBM) for x in (tokens, emission, dst_emb)])

    paired = rows == 8 and cols == 4
    if paired:
        half = rows // 2
        srcs = [src_emb, hop(src_emb, "row", rows, 1)]
        alphas = [alpha_prev, hop(alpha_prev, "row", rows, 1)]
        ready = lax.optimization_barrier((packed, srcs[1]))
        srcs[1] = ready[1]
        like = [packed] + [hop(ready[0], "row", rows, 2 * m) for m in range(1, half)]
        pile = pl.pallas_call(
            stack,
            out_shape=jax.ShapeDtypeStruct((half,) + packed.shape, packed.dtype),
            in_specs=[pl.BlockSpec(memory_space=VMEM)] * half,
            out_specs=pl.BlockSpec(memory_space=VMEM),
            name="stack",
            compiler_params=room(8),
        )(*like)
        arrived = [like, [hop(pile, "row", rows, 1)]]
        core = (lax.axis_index("row").astype(jnp.int32) & 1).reshape(1)
        sums_shape = (jax.ShapeDtypeStruct((2, seqs + TAIL, group), f32),) * 3
        sums_block = [((2, seqs + TAIL, group), False)] * 3
    else:
        srcs, alphas = [src_emb], [alpha_prev]
        arrived = [[lax.all_gather(packed, "row", axis=0)]]
        sums_shape = (jax.ShapeDtypeStruct((rows, seqs + TAIL, group), f32),)
        sums_block = [((rows, seqs + TAIL, group), False)]

    halves, tiles = len(srcs), len(arrived)
    wide = halves * sources
    tile_rows = rows // tiles
    per_step = math.gcd(tile_rows, 8)
    steps = tile_rows // per_step
    grid = (steps,) if steps > 1 else ()
    dst_block = ((per_step, depth + seqs, group), True)
    expo_block = ((per_step, group, wide), True)
    peak_block = ((tile_rows, wide), False)
    stat_block = ((2, wide), False)
    expos, peaks, stats = [], [], []
    for blocks in arrived:
        expo, peak, stat = pl.pallas_call(
            functools.partial(softmax_tile, steps, per_step, halves, len(blocks)),
            out_shape=(
                jax.ShapeDtypeStruct((tile_rows, group, wide), jnp.bfloat16),
                jax.ShapeDtypeStruct((tile_rows, wide), f32),
                jax.ShapeDtypeStruct((2, wide), f32),
            ),
            grid=grid,
            in_specs=block_specs(
                steps,
                [((sources, depth), False)] * halves + [dst_block] * len(blocks) + [stat_block] * len(stats),
            ),
            out_specs=block_specs(steps, [expo_block, peak_block, stat_block]),
            name="softmax_tile",
            compiler_params=room(16),
        )(*srcs, *blocks, *stats)
        expos.append(expo)
        peaks.append(peak)
        stats = [stat]

    known, _ = exchange(stats[0], rows, cols, paired)
    flat = sum(arrived, [])
    partial = pl.pallas_call(
        functools.partial(carry_tile, steps, per_step * tiles, cols, halves, tiles, len(sums_shape)),
        out_shape=sums_shape,
        grid=grid,
        in_specs=[pl.BlockSpec(memory_space=SMEM)] * paired
        + block_specs(
            steps,
            [stat_block] * cols
            + [((seqs, sources), False)] * halves
            + [expo_block] * tiles
            + [peak_block] * tiles
            + [dst_block] * len(flat),
        ),
        out_specs=block_specs(steps, sums_block),
        scratch_shapes=[pltpu.VMEM((group, group), f32)],
        name="carry_tile",
        compiler_params=room(16),
    )(*([core] if paired else []), *known, *alphas, *expos, *peaks, *flat)

    if paired:
        own, corner, turned = partial
        asked = lax.ppermute(turned, "row", [(i, i ^ (4 if i % 2 else 2)) for i in range(rows)])
        corner = hop(corner, "row", rows, rows - 2)
        told = hop(asked, "row", rows, 1)
        body, operands = emit_pair, (own, corner, asked, told, packed, arrived[1][0])
        block_shape = (2, seqs + TAIL, group)
    else:
        body, operands = emit_block, (lax.all_to_all(partial[0], "row", 0, 0), packed)
        block_shape = (seqs + TAIL, group)
    block = pl.pallas_call(
        body,
        out_shape=jax.ShapeDtypeStruct(block_shape, f32),
        in_specs=[pl.BlockSpec(memory_space=VMEM)] * len(operands),
        out_specs=pl.BlockSpec(memory_space=VMEM),
        name="emit_block",
        compiler_params=room(8),
    )(*operands)

    blocks, places = exchange(block, rows, cols, paired)
    return pl.pallas_call(
        functools.partial(finish, float(group * rows * cols), cols),
        out_shape=(jax.ShapeDtypeStruct((seqs, group * cols), f32), jax.ShapeDtypeStruct((seqs,), f32)),
        in_specs=[pl.BlockSpec(memory_space=SMEM)] * cols + [pl.BlockSpec(memory_space=VMEM)] * cols,
        out_specs=(pl.BlockSpec(memory_space=VMEM), pl.BlockSpec(memory_space=VMEM)),
        name="finish",
        compiler_params=room(8),
    )(*[p.reshape(1) for p in places], *blocks)


def solution(mesh):
    placed = (P(None, "row"), P(), P("row", None), P(None, ("row", "col")), P(None, ("row", "col")))
    return jax.shard_map(
        on_device, mesh=mesh, in_specs=placed, out_specs=(P(None, "row"), P()), check_vma=False
    )
```
